32 devices in a mesh: member: 2 (over x), slab: 16 (over z, y, core).
Axes of the slice: x: 2, y: 2, z: 4, core: 2. Of those that a mesh axis runs over, the one named last changes fastest.
Arguments:
- prior_ensemble_fields: float32 [64, 6, 128, 1, 1024], P('member', None, 'slab'), may hold values from -6 to 6
- params: float32 [64, 12], P('member'), may hold values from -3 to 3
- influence: int32 [12, 6], replicated, may hold values 0 or 1
- obs_cell: int32 [128, 2, 128], P('slab', 'member'), may hold values from 0 to 3071
- obs_value: float32 [128, 2, 128], P('slab', 'member'), may hold values from -6 to 6
- obs_prec: float32 [128, 2, 128], P('slab', 'member'), may hold values from 0.5 to 4
- cutoff: int32 [128], P('slab'), may hold values from 4 to 8, as said below
Outputs:
- analysis: bfloat16 [64, 6, 128, 1, 1024], P('member', None, 'slab')
- param_analysis: float32 [64, 12], P('member')
The draws below stay inside these ranges and needn't reach their ends.
Inputs may be any that keep to these rules, and one draw needn't show every extreme that they name: `obs_cell`: index = field * 512 + level * 512 + column within the block. `cutoff`: 8 is reached by some rows.
All inputs are finite; a program needn't handle non-finite values.
Results may differ from the reference program's by a relative error of at most 0.0056.
Values may be sent and summed in bfloat16 or wider, within the bound.
No kernel may reach another device: no remote copies, remote signals or barrier semaphores. Data moves between devices by JAX's collectives and lax.ppermute only.
A program may use at most 128 MiB of HBM per device.

```python
import math
import jax
import jax.numpy as jnp
from jax import lax

ENS = 64
FIELDS = 6
NPAR = 12
LEV = 1
COLS = 1024
HALO = 8
NOBS = 128
STEPS = 4
NS_STEPS = 5
NY = 128
NBLK = 2
CB = 512


def draw_cutoff(key, part):
    first_key = jax.random.fold_in(key, 11)
    second_key = jax.random.fold_in(key, 23)
    values = jax.random.randint(first_key, (NY,), HALO // 2, HALO + 1)
    order = jax.random.permutation(second_key, NY)
    chosen = order[:max(1, NY // 8)]
    values = values.at[chosen].set(HALO)
    return values.astype(jnp.int32)


def set_ends(entries, rng, smallest, largest):
    extent = entries.shape
    index_at = [jax.random.randint(jax.random.fold_in(rng, axis), (), 0, extent[axis]) for axis in range(len(extent))]
    entries = entries.at[tuple(index_at)].set(smallest)
    longest = extent.index(max(extent))
    index_at[longest] = (index_at[longest] + 1) % extent[longest]
    return entries.at[tuple(index_at)].set(largest)


def steps_of(stream_key, extent, split, smallest, largest):
    gain = 1.0
    for position, shards_of in split:
        heights = jax.random.uniform(jax.random.fold_in(jax.random.fold_in(stream_key, 6), position), (shards_of,), jnp.float32, smallest / len(split), largest / len(split))
        gain = gain * jnp.repeat(jnp.exp(heights), extent[position] // shards_of).reshape((-1,) + (1,) * (len(extent) - 1 - position))
    return gain


def noise(rng, dims, deviation, reach, shards=(), kind=jnp.bfloat16):
    array = deviation * jax.random.normal(rng, dims, jnp.float32)
    if shards:
        array = array * steps_of(rng, dims, shards, -0.22, 0.18)
    return jnp.clip(array, -reach, reach).astype(kind)


def setup_inputs(seed: int = 0) -> dict:
    keys = jax.random.split(jax.random.key(seed), 8)
    return {
        "prior_ensemble_fields": noise(keys[0], (ENS, FIELDS, NY, LEV, COLS), 1.0, 6.0, ((0, 2), (2, 16)), jnp.float32),
        "params": noise(keys[1], (ENS, NPAR), 0.5, 3.0, ((0, 2),), jnp.float32),
        "influence": set_ends((jax.random.randint(keys[2], (NPAR, FIELDS), 0, 2) < 1).astype(jnp.int32), jax.random.fold_in(keys[2], 1), 0, 1),
        "obs_cell": set_ends(jax.random.randint(keys[3], (NY, NBLK, NOBS), 0, FIELDS * LEV * CB), jax.random.fold_in(keys[3], 1), 0, (FIELDS * LEV * CB) - 1).astype(jnp.int32),
        "obs_value": noise(keys[4], (NY, NBLK, NOBS), 1.5, 6.0, ((0, 16), (1, 2)), jnp.float32),
        "obs_prec": jnp.clip(jnp.exp(math.log(4.0) - 2.0794415 * jax.random.uniform(keys[5], (NY, NBLK, NOBS), jnp.float32) ** steps_of(keys[5], (NY, NBLK, NOBS), ((0, 16), (1, 2)), -0.2, 0.2)), 0.5, 4.0),
        "cutoff": draw_cutoff(jax.random.fold_in(keys[7], 71), 0),
    }


diffusion = 0.2
advection = 0.15
vertical = 0.1
coupling = 0.2

def stencil_step(prognostic_vector, coef_row):
    zero_row = jnp.zeros_like(prognostic_vector[:, :1])
    upper = jnp.concatenate([prognostic_vector[:, 1:], zero_row], 1)
    lower = jnp.concatenate([zero_row, prognostic_vector[:, :-1]], 1)
    right_col = jnp.roll(prognostic_vector, -1, 3)
    left_col = jnp.roll(prognostic_vector, 1, 3)
    laplace = upper + lower + right_col + left_col - 4.0 * prognostic_vector
    return prognostic_vector + diffusion * laplace - advection * (right_col - left_col) + vertical * (jnp.roll(prognostic_vector, 1, 2) - prognostic_vector) + coupling * coef_row[:, None, None, None] * jnp.roll(prognostic_vector, -1, 0)

def propagate_single_trajectory(incoming_grids):
    prognostic_vector, coef_row = incoming_grids
    for step_idx in range(STEPS):
        prognostic_vector = stencil_step(prognostic_vector, coef_row)
    return prognostic_vector.astype(jnp.bfloat16)

def newton_roots(amat):
    highest = lax.Precision.HIGHEST
    ensemble = amat.shape[-1]
    eye_mat = jnp.eye(ensemble, dtype=jnp.float32)
    scale = jnp.sqrt(lax.optimization_barrier(jnp.sum(amat * amat, axis=(-2, -1))))
    ymat = amat / scale[..., None, None]
    zmat = jnp.broadcast_to(eye_mat, amat.shape)
    for step_idx in range(NS_STEPS):
        middle = 1.5 * eye_mat - 0.5 * jnp.matmul(zmat, ymat, precision=highest)
        ymat = jnp.matmul(ymat, middle, precision=highest)
        zmat = jnp.matmul(middle, zmat, precision=highest)
    return (zmat, scale)

def reference(prior_ensemble_fields, params, influence, obs_cell, obs_value, obs_prec, cutoff):
    highest = lax.Precision.HIGHEST
    dynamics_parameter = jnp.dot(params, influence.astype(jnp.float32), precision=highest)
    propagate_timestep = lax.map(propagate_single_trajectory, (prior_ensemble_fields, dynamics_parameter))

    def row_gram(latitude_offset):
        band_prognostic_entries = lax.dynamic_index_in_dim(propagate_timestep, latitude_offset, 2, keepdims=False).astype(jnp.float32)
        band_prognostic_entries = band_prognostic_entries.reshape(ENS, FIELDS, LEV, NBLK, CB)
        cells = lax.dynamic_index_in_dim(obs_cell, latitude_offset, 0, keepdims=False)
        values = lax.dynamic_index_in_dim(obs_value, latitude_offset, 0, keepdims=False)
        precs = lax.dynamic_index_in_dim(obs_prec, latitude_offset, 0, keepdims=False)
        kinds = cells // (LEV * CB)
        levels = cells // CB % LEV
        columns = cells % CB
        blocks = jnp.arange(NBLK, dtype=jnp.int32)[:, None]
        ens_obs = band_prognostic_entries[:, kinds, levels, blocks, columns]
        ybar = lax.optimization_barrier(jnp.mean(ens_obs, axis=0))
        ypert = ens_obs - ybar
        weighted = precs * (values - ybar)
        gram = jnp.einsum('ebo,fbo->bef', ypert * precs[None], ypert, precision=highest)
        gvec = jnp.einsum('ebo,bo->be', ypert, weighted, precision=highest)
        return jnp.concatenate([gram, gvec[:, None, :]], 1)
    stacked = lax.map(row_gram, jnp.arange(NY, dtype=jnp.int32))
    padded = jnp.pad(stacked, ((HALO, HALO), (0, 0), (0, 0), (0, 0)))
    radius = cutoff.astype(jnp.float32)
    local = jnp.zeros_like(stacked)
    for offset in range(-HALO, HALO + 1):
        weight = jnp.maximum(0.0, 1.0 - abs(offset) / (radius + 1.0))
        local = local + weight[:, None, None, None] * padded[HALO + offset:HALO + offset + NY]
    gram_loc = local[:, :, :ENS]
    gvec_loc = local[:, :, ENS]
    amat = (ENS - 1.0) * jnp.eye(ENS, dtype=jnp.float32) + gram_loc
    zmat, scale = newton_roots(amat)
    wpert = math.sqrt(ENS - 1.0) * zmat / jnp.sqrt(scale)[..., None, None]
    inner = jnp.matmul(zmat, gvec_loc[..., None], precision=highest)
    wbar = jnp.matmul(zmat, inner, precision=highest)[..., 0] / scale[..., None]
    weights = wpert + wbar[..., None]

    def row_update(incoming_grids):
        latitude_offset, row_weights = incoming_grids
        band_prognostic_entries = lax.dynamic_index_in_dim(propagate_timestep, latitude_offset, 2, keepdims=False).astype(jnp.float32)
        band_prognostic_entries = band_prognostic_entries.reshape(ENS, FIELDS, LEV, NBLK, CB)
        xbar = lax.optimization_barrier(jnp.mean(band_prognostic_entries, axis=0))
        xpert = band_prognostic_entries - xbar
        update = jnp.einsum('jflbc,bje->eflbc', xpert, row_weights, precision=highest)
        return (xbar + update).astype(jnp.bfloat16).reshape(ENS, FIELDS, LEV, COLS)
    rows_out = lax.map(row_update, (jnp.arange(NY, dtype=jnp.int32), weights))
    analysis = jnp.moveaxis(rows_out, 0, 2)
    wmean = lax.optimization_barrier(jnp.sum(weights, axis=(0, 1))) / (NY * NBLK)
    pbar = lax.optimization_barrier(jnp.mean(params, axis=0))
    ppert = params - pbar
    param_analysis = pbar + jnp.einsum('jk,je->ek', ppert, wmean, precision=highest)
    return (analysis, param_analysis)
```

```python
import math

import jax
import jax.numpy as jnp
from jax import lax
from jax.experimental import pallas as pl
from jax.experimental.pallas import tpu as pltpu
from jax.sharding import PartitionSpec as P


HALO = 8
STEPS = 4
NS_STEPS = 5
LANES = 128
TILE = 8

diffusion = 0.2
advection = 0.15
vertical = 0.1
coupling = 0.2


def planes_of(fields, levels):
    return [(f, l) for f in range(fields) for l in range(levels)]


def pack_kernel(fields, rows, levels, cols, count, odd_ref, x_ref, *rest):
    outs, turned, edges, sems = rest[:2 * count + 1], *rest[2 * count + 1:]
    groups = cols // LANES
    stride = fields * rows * levels * groups
    planes = fields * levels
    tile = pl.program_id(0)

    def row(y, _):
        for p, (f, l) in enumerate(planes_of(fields, levels)):
            for s in range(groups):
                start = ((f * rows + y) * levels + l) * groups + s
                turned[tile, p, y, :, s * LANES:(s + 1) * LANES] = x_ref[pl.ds(start, TILE, stride=stride), :]
        return 0

    lax.fori_loop(0, rows, row, 0)

    def edge(y, _):
        for side in range(2):
            at = jnp.where(odd_ref[0] == side, rows - STEPS, 0) + y
            for p in range(planes):
                edges[tile, side, p, y] = turned[tile, p, at].astype(jnp.bfloat16)
        return 0

    lax.fori_loop(0, STEPS, edge, 0)

    def copies(k):
        pairs = [(edges.at[k, 0], outs[2 * k]), (edges.at[k, 1], outs[2 * k + 1]), (turned.at[k], outs[-1].at[k])]
        return [pltpu.make_async_copy(src, dst, sems.at[k, i]) for i, (src, dst) in enumerate(pairs)]

    for k in range(count):
        @pl.when(tile == k)
        def _():
            for copy in copies(k):
                copy.start()

    @pl.when(tile == count - 1)
    def _():
        for k in range(count):
            for copy in copies(k):
                copy.wait()


def pack(odd, x2, first, count, fields, rows, levels, cols):
    planes = fields * levels
    block = TILE * fields * rows * levels * cols // LANES
    edge = (planes, STEPS, TILE, cols)
    turned = (count, planes, rows, TILE, cols)
    return pl.pallas_call(
        lambda *refs: pack_kernel(fields, rows, levels, cols, count, *refs),
        grid=(count,),
        in_specs=[pl.BlockSpec(memory_space=pltpu.SMEM), pl.BlockSpec((block, LANES), lambda i: (first + i, 0))],
        out_specs=[pl.BlockSpec(memory_space=pl.ANY)] * (2 * count + 1),
        out_shape=[jax.ShapeDtypeStruct(edge, jnp.bfloat16)] * (2 * count) + [jax.ShapeDtypeStruct(turned, jnp.float32)],
        scratch_shapes=[
            pltpu.VMEM(turned, jnp.float32),
            pltpu.VMEM((count, 2, *edge), jnp.bfloat16),
            pltpu.SemaphoreType.DMA((count, 3)),
        ],
        name="pack",
    )(odd, x2)


def stencil_kernel(fields, rows, levels, cols, blocks, splits, local, odd_ref, open_ref, x_ref, first_ref, second_ref, coef_ref, cell_ref, *rest):
    out_refs = rest[:len(splits)]
    obs_ref = rest[len(splits)]
    *state, mixed, sem = rest[len(splits) + 1:]
    groups = cols // LANES
    block_cols = cols // blocks
    pairs = planes_of(fields, levels)
    planes = len(pairs)

    own_copy = pltpu.make_async_copy(x_ref.at[local], state[0].at[:, pl.ds(STEPS, rows)], sem)
    own_copy.start()

    def tile_at(s):
        return slice(s * LANES, (s + 1) * LANES)

    odd = odd_ref[0] == 1

    def load_edge(y, _):
        for p in range(planes):
            first = first_ref[p, y].astype(jnp.float32)
            second = second_ref[p, y].astype(jnp.float32)
            state[0][p, y] = jnp.where(odd, first, second)
            state[0][p, STEPS + rows + y] = jnp.where(odd, second, first)
        return 0

    lax.fori_loop(0, STEPS, load_edge, 0)
    own_copy.wait()

    lane = lax.broadcasted_iota(jnp.int32, (TILE, LANES), 1)
    at_last = lane == LANES - 1
    at_first = lane == 0
    centre = (1.0 - 4.0 * diffusion - vertical) / diffusion
    below_part = vertical / diffusion
    right_part = (diffusion - advection) / diffusion
    left_part = (diffusion + advection) / diffusion
    next_part = coupling / diffusion
    scale = diffusion ** STEPS
    coefs = [next_part * coef_ref[0, f] for f in range(fields)]

    def rest_of_step(src, y, p):
        f, l = pairs[p]
        after = ((f + 1) % fields) * levels + l
        under = f * levels + (l - 1) % levels
        mid, out = [], []
        for s in range(groups):
            here = src[p, y, :, tile_at(s)]
            around = src[p, y + 1, :, tile_at(s)] + src[p, y - 1, :, tile_at(s)]
            if under == p:
                whole = centre + below_part
                own = here if abs(whole - 1.0) < 1e-12 else whole * here
            else:
                own = centre * here + below_part * src[under, y, :, tile_at(s)]
            mid.append(here)
            out.append((around + own) + coefs[f] * src[after, y, :, tile_at(s)])
        return mid, out

    pace = 2 if rows % 2 == 0 else 1
    for t in range(1, STEPS + 1):
        src, dst = state[(t - 1) % 2], state[t % 2]
        reach = STEPS - t
        ratio = math.comb(STEPS, t - 1) / math.comb(STEPS, t)

        def edge_rows(i, _):
            for side, y in enumerate((t + i, STEPS + rows + i)):
                for p in range(planes):
                    for s, value in enumerate(rest_of_step(src, y, p)[1]):
                        dst[p, y, :, tile_at(s)] = value * open_ref[side]
            return 0

        def own_rows(i, _):
            for k in range(pace):
                mine = pace * i + k
                for p in range(planes):
                    mid, out = rest_of_step(src, STEPS + mine, p)
                    if t > 1:
                        mid = [mixed[p, mine, :, tile_at(s)] for s in range(groups)]
                    ahead = [pltpu.roll(v, LANES - 1, 1) for v in mid]
                    behind = [pltpu.roll(v, 1, 1) for v in mid]
                    for s in range(groups):
                        right = jnp.where(at_last, ahead[(s + 1) % groups], ahead[s])
                        left = jnp.where(at_first, behind[(s - 1) % groups], behind[s])
                        value = out[s] + (ratio * right_part * right + ratio * left_part * left)
                        if t < STEPS:
                            dst[p, STEPS + mine, :, tile_at(s)] = out[s]
                            mixed[p, mine, :, tile_at(s)] = value
                            continue
                        value = value * scale
                        mixed[p, mine, :, tile_at(s)] = value
                        for g, (start, count) in enumerate(splits):
                            if start <= p < start + count:
                                at = pl.ds(pl.multiple_of(mine * TILE, TILE), TILE)
                                out_refs[g][p - start, s, at, :] = value.astype(jnp.bfloat16)
            return 0

        if reach:
            lax.fori_loop(0, reach, edge_rows, 0)
        lax.fori_loop(0, rows // pace, own_rows, 0)

    column = lax.broadcasted_iota(jnp.int32, (block_cols, LANES), 0)

    def observe(i, _):
        for k in range(pace):
            y = pace * i + k
            for b in range(blocks):
                cell = cell_ref[y, b:b + 1, :]
                plane = cell // block_cols
                pick = jnp.where(column == cell - plane * block_cols, 1.0, 0.0).astype(jnp.bfloat16)
                part = mixed[:, y, :, b * block_cols:(b + 1) * block_cols]
                part = part.reshape(planes * TILE, block_cols).astype(jnp.bfloat16)
                found = jnp.dot(part, pick, preferred_element_type=jnp.float32).reshape(planes, TILE, LANES)
                total = jnp.zeros((TILE, LANES), jnp.float32)
                for p in range(planes):
                    total = jnp.where(plane == p, found[p], total)
                obs_ref[y, b] = total.astype(jnp.bfloat16)
        return 0

    lax.fori_loop(0, rows // pace, observe, 0)


def stencil(odd, inside, turned, first, second, coef, cells, tile, local, splits, fields, rows, levels, cols):
    planes = fields * levels
    blocks = cells.shape[1]
    outs = [jax.ShapeDtypeStruct((count, cols // LANES, rows * TILE, LANES), jnp.bfloat16) for _, count in splits]
    outs.append(jax.ShapeDtypeStruct((rows, blocks, TILE, LANES), jnp.bfloat16))
    room = pltpu.VMEM((planes, rows + 2 * STEPS, TILE, cols), jnp.float32)

    def all_of(shape):
        return pl.BlockSpec(shape, lambda i: (0,) * len(shape))

    return pl.pallas_call(
        lambda *refs: stencil_kernel(fields, rows, levels, cols, blocks, splits, local, *refs),
        grid=(1,),
        in_specs=[
            pl.BlockSpec(memory_space=pltpu.SMEM),
            pl.BlockSpec(memory_space=pltpu.SMEM),
            pl.BlockSpec(memory_space=pl.ANY),
            all_of(first.shape),
            all_of(second.shape),
            pl.BlockSpec((1, fields, TILE, LANES), lambda i: (tile, 0, 0, 0)),
            all_of(cells.shape),
        ],
        out_specs=[all_of(out.shape) for out in outs],
        out_shape=outs,
        scratch_shapes=[room, room, pltpu.VMEM((planes, rows, TILE, cols), jnp.float32), pltpu.SemaphoreType.DMA],
        name="stencil",
    )(odd, inside, turned, first, second, coef, cells)


def spread_kernel(members, rows, blocks, depth, w_ref, upper_ref, lower_ref):
    ensemble = w_ref.shape[2]
    member = lax.broadcasted_iota(jnp.int32, (ensemble, depth), 0)
    column = lax.broadcasted_iota(jnp.int32, (ensemble, depth), 1)
    place = jnp.where(member == column // (rows * TILE) * TILE + column % TILE, 1.0, 0.0).astype(jnp.bfloat16)
    mine = lax.broadcasted_iota(jnp.int32, (members * rows, depth), 0) % rows
    theirs = lax.broadcasted_iota(jnp.int32, (members * rows, depth), 1) // TILE % rows
    keep = mine == theirs
    for b in range(blocks):
        w = w_ref[b]
        high = w.astype(jnp.bfloat16)
        low = (w - high.astype(jnp.float32)).astype(jnp.bfloat16)
        for part, ref in ((high, upper_ref), (low, lower_ref)):
            wide = jnp.dot(part, place, preferred_element_type=jnp.float32)
            ref[b] = jnp.where(keep, wide, 0.0).astype(jnp.bfloat16)


def spread(w, members, rows):
    blocks, _, ensemble = w.shape
    depth = ensemble * rows
    out = jax.ShapeDtypeStruct((blocks, members * rows, depth), jnp.bfloat16)
    return pl.pallas_call(
        lambda *refs: spread_kernel(members, rows, blocks, depth, *refs),
        out_shape=[out, out],
        name="spread",
    )(w)


def update_kernel(members, rows, cols, blocks, count, upper, lower, *rest):
    pieces, out_ref = rest[:count], rest[-1]
    groups = cols // blocks // LANES
    for b in range(blocks):
        columns = []
        for s in range(b * groups, (b + 1) * groups):
            columns.append(jnp.concatenate([piece[0, s] for piece in pieces], axis=0))
        x = jnp.concatenate(columns, axis=1) if groups > 1 else columns[0]
        total = jnp.dot(upper[b], x, preferred_element_type=jnp.float32)
        total = total + jnp.dot(lower[b], x, preferred_element_type=jnp.float32)
        total = total.reshape(members, rows, groups * LANES).astype(jnp.bfloat16)
        out_ref[:, 0, :, b * groups * LANES:(b + 1) * groups * LANES] = total


def update(upper, lower, pieces, offsets, start, count, held, members, planes, rows, cols):
    blocks = upper.shape[0]

    def piece_spec(piece, offset):
        return pl.BlockSpec((1, *piece.shape[1:]), lambda i: (offset + i, 0, 0, 0))

    in_specs = [pl.BlockSpec(upper.shape, lambda i: (0, 0, 0))] * 2
    in_specs += [piece_spec(piece, offset) for piece, offset in zip(pieces, offsets)]
    args = [upper, lower, *pieces]
    aliases = {}
    if held is not None:
        aliases = {len(args): 0}
        in_specs.append(pl.BlockSpec(memory_space=pl.ANY))
        args.append(held)
    return pl.pallas_call(
        lambda *refs: update_kernel(members, rows, cols, blocks, len(pieces), *refs),
        grid=(count,),
        in_specs=in_specs,
        out_specs=pl.BlockSpec((members, 1, rows, cols), lambda i: (0, start + i, 0, 0)),
        out_shape=jax.ShapeDtypeStruct((members, planes, rows, cols), jnp.bfloat16),
        input_output_aliases=aliases,
        name="update",
    )(*args)


def from_member(array, shift):
    count = lax.axis_size("member")
    return lax.ppermute(array, "member", [((i + shift) % count, i) for i in range(count)])


def all_members(array):
    return [array] + [from_member(array, shift) for shift in range(1, lax.axis_size("member"))]


def swap_one(array):
    return lax.ppermute(array, "slab", [(i, i ^ 1) for i in range(lax.axis_size("slab"))])


def swap_two(array):
    pairs = [(i, i + 1) for i in range(1, lax.axis_size("slab") - 1, 2)]
    return lax.ppermute(array, "slab", pairs + [(j, i) for i, j in pairs])


def groups_of(planes):
    sizes = [2] * (planes // 2 - 1) + [1, 1] if planes % 2 == 0 else [1] * planes
    return [(sum(sizes[:i]), size) for i, size in enumerate(sizes)]


def cycle(prior_ensemble_fields, params, influence, obs_cell, obs_value, obs_prec, cutoff):
    highest = lax.Precision.HIGHEST
    fine_grain = lax.Precision.HIGH
    members, fields, rows, levels, cols = prior_ensemble_fields.shape
    planes = fields * levels
    tiles = members // TILE
    devices = lax.axis_size("member")
    slabs = lax.axis_size("slab")
    ensemble = members * devices
    me = lax.axis_index("member")
    place = lax.axis_index("slab")
    dims = (fields, rows, levels, cols)
    x2 = prior_ensemble_fields.reshape(members * fields * rows * levels * (cols // LANES), LANES)

    odd = (place % 2).astype(jnp.int32).reshape(1)

    *packed, turned = pack(odd, x2, 0, 1, *dims)
    turned = [(turned, 0)]
    if tiles > 1:
        *more, others = pack(odd, x2, 1, tiles - 1, *dims)
        packed += more
        turned += [(others, i) for i in range(tiles - 1)]
    edges = []
    for i in range(tiles):
        edges.append((swap_one(packed[2 * i]), swap_two(packed[2 * i + 1])))

    columns = obs_cell.shape[2]
    npar = params.shape[1]
    own_small = jnp.concatenate(
        [obs_cell[:, 0].astype(jnp.float32), obs_value[:, 0], obs_prec[:, 0]]
        + [jnp.pad(params.T, ((0, -npar % TILE), (0, columns - members)))]
    )
    small = jnp.stack(all_members(own_small))
    every_param = small[:, 3 * rows:3 * rows + npar, :members].transpose(0, 2, 1).reshape(ensemble, npar)
    every = jnp.concatenate([small[:, :3 * rows]] * 2)
    every = lax.dynamic_slice_in_dim(every, devices - me, devices, 0).reshape(devices, 3, rows, columns)
    cells = jnp.moveaxis(every[:, 0], 0, 1).astype(jnp.int32)
    values = jnp.moveaxis(every[:, 1], 0, 1)
    precs = jnp.moveaxis(every[:, 2], 0, 1)

    coef = jnp.dot(params, influence.astype(jnp.float32), precision=highest)
    coef = jnp.broadcast_to(coef.reshape(tiles, TILE, fields).transpose(0, 2, 1)[..., None], (tiles, fields, TILE, LANES))
    inside = jnp.stack([place > 0, place < slabs - 1]).astype(jnp.float32)

    fine = groups_of(planes)
    forecasts, observed = [], []
    for i in range(tiles):
        splits = fine if i == tiles - 1 else [(0, planes)]
        fields_here, local = turned[i]
        *outs, obs = stencil(odd, inside, fields_here, *edges[i], coef, cells, i, local, splits, *dims)
        forecasts.append(outs)
        observed.append(obs)
    ens_obs = jnp.stack(all_members(jnp.stack(observed)))
    sent = []
    for outs in forecasts:
        arrays = []
        for out in outs:
            arrays.append(all_members(out))
        sent.append(arrays)

    ens_obs = ens_obs.transpose(2, 3, 0, 1, 4, 5).reshape(rows, devices, ensemble, LANES).astype(jnp.float32)
    ybar = jnp.mean(ens_obs, axis=2, keepdims=True)
    ypert = ens_obs - ybar
    weighted = precs * (values - ybar[:, :, 0])
    gram = jnp.einsum("rbeo,rbfo->rbef", ypert * precs[:, :, None], ypert, precision=fine_grain)
    gvec = jnp.einsum("rbeo,rbo->rbe", ypert, weighted, precision=highest)
    stacked = jnp.concatenate([gram, gvec[:, :, None, :]], axis=2)
    stacked = jnp.concatenate([stacked[:, 0::2], stacked[:, 1::2]], axis=3)
    rounded = stacked.astype(jnp.bfloat16)
    near, far = swap_one(rounded), swap_two(rounded)
    near, far = near.astype(jnp.float32), far.astype(jnp.float32)
    is_odd = place % 2 == 1
    wide = jnp.concatenate([jnp.where(is_odd, near, far), stacked, jnp.where(is_odd, far, near)], axis=0)
    radius = cutoff.astype(jnp.float32)
    local = jnp.zeros_like(stacked)
    for offset in range(-HALO, HALO + 1):
        weight = jnp.maximum(0.0, 1.0 - abs(offset) / (radius + 1.0))
        local = local + weight[:, None, None, None] * wide[rows + offset:2 * rows + offset]
    local = jnp.stack([local[..., :ensemble], local[..., ensemble:]], axis=2).reshape(rows, devices, ensemble + 1, ensemble)
    gram_loc = local[:, :, :ensemble]
    gvec_loc = local[:, :, ensemble]
    eye_mat = jnp.eye(ensemble, dtype=jnp.float32)
    amat = (ensemble - 1.0) * eye_mat + gram_loc
    scale = jnp.sqrt(jnp.sum(amat * amat, axis=(2, 3)))[:, :, None, None]
    ymat = amat / scale
    zmat = None
    for _ in range(NS_STEPS):
        middle = 1.5 * eye_mat - 0.5 * (ymat if zmat is None else jnp.matmul(zmat, ymat, precision=fine_grain))
        ymat = jnp.matmul(ymat, middle, precision=fine_grain)
        zmat = middle if zmat is None else jnp.matmul(middle, zmat, precision=fine_grain)
    wpert = math.sqrt(ensemble - 1.0) * zmat / jnp.sqrt(scale)
    inner = jnp.matmul(zmat, gvec_loc[..., None], precision=highest)
    wbar = jnp.matmul(zmat, inner, precision=highest) / scale
    weights = (wpert + wbar)[..., :members]

    direct = weights + (1.0 - jnp.sum(weights, axis=2, keepdims=True)) / ensemble
    w = direct.transpose(1, 3, 0, 2).reshape(devices, members * rows, ensemble)

    upper, lower = spread(w, members, rows)

    analysis = None
    for g, (start, count) in enumerate(fine):
        pieces, offsets = [], []
        for r in range(devices):
            for arrays in sent:
                pieces.append(arrays[g if len(arrays) > 1 else 0][r])
                offsets.append(0 if len(arrays) > 1 else start)
        analysis = update(upper, lower, pieces, offsets, start, count, analysis, members, planes, rows, cols)
    analysis = analysis.reshape(members, fields, levels, rows, cols).transpose(0, 1, 3, 2, 4)

    pbar = jnp.mean(every_param, axis=0)
    ppert = every_param - pbar
    weight_rows = jnp.sum(weights, axis=(0, 1))
    part = jnp.einsum("jk,je->ke", ppert, weight_rows, precision=highest)
    step = 1
    while step < slabs:
        part = part + lax.ppermute(part, "slab", [(i, i ^ step) for i in range(slabs)])
        step *= 2
    total = part / (rows * slabs * devices)
    param_analysis = pbar + total.T
    return (analysis, param_analysis)


def solution(mesh):
    in_specs = (
        P("member", None, "slab", None, None),
        P("member", None),
        P(),
        P("slab", "member", None),
        P("slab", "member", None),
        P("slab", "member", None),
        P("slab"),
    )
    out_specs = (P("member", None, "slab", None, None), P("member", None))
    return jax.shard_map(cycle, mesh=mesh, in_specs=in_specs, out_specs=out_specs, check_vma=False)
```

```python
import math

import jax
import jax.numpy as jnp
from jax import lax
from jax.experimental import pallas as pl
from jax.experimental.pallas import tpu as pltpu
from jax.sharding import PartitionSpec as P


HALO = 8
STEPS = 4
NS_STEPS = 5
LANES = 128
TILE = 8
PACE = 4
KERNEL_VMEM = 44 * 1024 * 1024
ODD, ME, OPEN = 0, 1, 2

diffusion = 0.2
advection = 0.15
vertical = 0.1
coupling = 0.2


def planes_of(fields, levels):
    return [(f, l) for f in range(fields) for l in range(levels)]


def pack_kernel(fields, rows, levels, cols, count, flags_ref, x_ref, *rest):
    outs, turned, edges, sems = rest[:2 * count + 1], *rest[2 * count + 1:]
    groups = cols // LANES
    stride = fields * rows * levels * groups
    planes = fields * levels
    tile = pl.program_id(0)

    def row(y, _):
        for p, (f, l) in enumerate(planes_of(fields, levels)):
            for s in range(groups):
                start = ((f * rows + y) * levels + l) * groups + s
                turned[tile, p, y, :, s * LANES:(s + 1) * LANES] = x_ref[pl.ds(start, TILE, stride=stride), :]
        return 0

    lax.fori_loop(0, rows, row, 0)

    def edge(y, _):
        for side in range(2):
            at = jnp.where(flags_ref[ODD] == side, rows - STEPS, 0) + y
            for p in range(planes):
                edges[tile, side, p, y] = turned[tile, p, at].astype(jnp.bfloat16)
        return 0

    lax.fori_loop(0, STEPS, edge, 0)

    def copies(k):
        pairs = [(edges.at[k, 0], outs[2 * k]), (edges.at[k, 1], outs[2 * k + 1]), (turned.at[k], outs[-1].at[k])]
        return [pltpu.make_async_copy(src, dst, sems.at[k, i]) for i, (src, dst) in enumerate(pairs)]

    for k in range(count):
        @pl.when(tile == k)
        def _():
            for copy in copies(k):
                copy.start()

    @pl.when(tile == count - 1)
    def _():
        for k in range(count):
            for copy in copies(k):
                copy.wait()


def pack(flags, x2, first, count, fields, rows, levels, cols):
    planes = fields * levels
    block = TILE * fields * rows * levels * cols // LANES
    edge = (planes, STEPS, TILE, cols)
    turned = (count, planes, rows, TILE, cols)
    return pl.pallas_call(
        lambda *refs: pack_kernel(fields, rows, levels, cols, count, *refs),
        grid=(count,),
        in_specs=[pl.BlockSpec(memory_space=pltpu.SMEM), pl.BlockSpec((block, LANES), lambda i: (first + i, 0))],
        out_specs=[pl.BlockSpec(memory_space=pltpu.HBM)] * (2 * count + 1),
        out_shape=[jax.ShapeDtypeStruct(edge, jnp.bfloat16)] * (2 * count) + [jax.ShapeDtypeStruct(turned, jnp.float32)],
        scratch_shapes=[
            pltpu.VMEM(turned, jnp.float32),
            pltpu.VMEM((count, 2, *edge), jnp.bfloat16),
            pltpu.SemaphoreType.DMA((count, 3)),
        ],
        name="pack",
    )(flags, pltpu.with_memory_space_constraint(x2, pltpu.HBM))


def stencil_kernel(fields, rows, levels, cols, blocks, splits, local, held, flags_ref, x_ref, first_ref, second_ref, coef_ref, *rest):
    small_refs, rest = rest[:blocks], rest[blocks + held:]
    out_refs = rest[:len(splits)]
    obs_ref = rest[len(splits)]
    *state, mixed, sem = rest[len(splits) + 1:]
    groups = cols // LANES
    block_cols = cols // blocks
    pairs = planes_of(fields, levels)
    planes = len(pairs)

    own_copy = pltpu.make_async_copy(x_ref.at[local], state[0].at[:, pl.ds(STEPS, rows)], sem)
    own_copy.start()

    def tile_at(s):
        return slice(s * LANES, (s + 1) * LANES)

    odd = flags_ref[ODD] == 1

    def load_edge(y, _):
        for p in range(planes):
            first = first_ref[p, y].astype(jnp.float32)
            second = second_ref[p, y].astype(jnp.float32)
            state[0][p, y] = jnp.where(odd, first, second)
            state[0][p, STEPS + rows + y] = jnp.where(odd, second, first)
        return 0

    lax.fori_loop(0, STEPS, load_edge, 0)
    own_copy.wait()
    is_open = [flags_ref[OPEN + side].astype(jnp.float32) for side in range(2)]

    lane = lax.broadcasted_iota(jnp.int32, (TILE, LANES), 1)
    at_last = lane == LANES - 1
    at_first = lane == 0
    centre = (1.0 - 4.0 * diffusion - vertical) / diffusion
    below_part = vertical / diffusion
    right_part = (diffusion - advection) / diffusion
    left_part = (diffusion + advection) / diffusion
    next_part = coupling / diffusion
    scale = diffusion ** STEPS
    coefs = [jnp.broadcast_to(next_part * coef_ref[:, f:f + 1], (TILE, LANES)) for f in range(fields)]

    def rest_of_step(src, y, p):
        f, l = pairs[p]
        after = ((f + 1) % fields) * levels + l
        under = f * levels + (l - 1) % levels
        mid, out = [], []
        for s in range(groups):
            here = src[p, y, :, tile_at(s)]
            around = src[p, y + 1, :, tile_at(s)] + src[p, y - 1, :, tile_at(s)]
            if under == p:
                whole = centre + below_part
                own = here if abs(whole - 1.0) < 1e-12 else whole * here
            else:
                own = centre * here + below_part * src[under, y, :, tile_at(s)]
            mid.append(here)
            out.append((around + own) + coefs[f] * src[after, y, :, tile_at(s)])
        return mid, out

    def shifted(tiles):
        moved = []
        for s in range(0, groups, 2):
            both = jnp.concatenate(tiles[s:s + 2], axis=0).astype(jnp.bfloat16)
            both = pltpu.roll(both, LANES - 1, 1).astype(jnp.float32)
            moved += [both[k:k + TILE] for k in range(0, both.shape[0], TILE)]
        return moved

    pace = PACE if rows % PACE == 0 else 1
    for t in range(1, STEPS + 1):
        src, dst = state[(t - 1) % 2], state[t % 2]
        reach = STEPS - t
        ratio = math.comb(STEPS, t - 1) / math.comb(STEPS, t)

        def edge_rows(i, _):
            for side, y in enumerate((t + i, STEPS + rows + i)):
                for p in range(planes):
                    for s, value in enumerate(rest_of_step(src, y, p)[1]):
                        dst[p, y, :, tile_at(s)] = value * is_open[side]
            return 0

        def own_rows(i, _):
            for k in range(pace):
                mine = pace * i + k
                for p in range(planes):
                    mid, out = rest_of_step(src, STEPS + mine, p)
                    if t > 1:
                        mid = [mixed[p, mine, :, tile_at(s)] for s in range(groups)]
                    ahead = shifted(mid)
                    behind = [pltpu.roll(v, 1, 1) for v in mid]
                    for s in range(groups):
                        right = jnp.where(at_last, ahead[(s + 1) % groups], ahead[s])
                        left = jnp.where(at_first, behind[(s - 1) % groups], behind[s])
                        value = out[s] + (ratio * right_part * right + ratio * left_part * left)
                        if t < STEPS:
                            dst[p, STEPS + mine, :, tile_at(s)] = out[s]
                            mixed[p, mine, :, tile_at(s)] = value
                            continue
                        value = value * scale
                        mixed[p, mine, :, tile_at(s)] = value
                        for g, (start, count) in enumerate(splits):
                            if start <= p < start + count:
                                at = pl.ds(pl.multiple_of(mine * TILE, TILE), TILE)
                                out_refs[g][p - start, s, at, :] = value.astype(jnp.bfloat16)
            return 0

        if reach:
            lax.fori_loop(0, reach, edge_rows, 0)
        lax.fori_loop(0, rows // pace, own_rows, 0)

    column = lax.broadcasted_iota(jnp.int32, (block_cols, LANES), 0)

    def observe(i, _):
        for k in range(pace):
            y = pace * i + k
            for b in range(blocks):
                cell = small_refs[b][pl.ds(y, 1), :].astype(jnp.int32)
                plane = cell // block_cols
                pick = jnp.where(column == cell - plane * block_cols, 1.0, 0.0).astype(jnp.bfloat16)
                start = (flags_ref[ME] + b) % blocks * block_cols
                part = mixed[:, y, :, pl.ds(pl.multiple_of(start, LANES), block_cols)]
                part = part.reshape(planes * TILE, block_cols).astype(jnp.bfloat16)
                found = jnp.dot(part, pick, preferred_element_type=jnp.float32).reshape(planes, TILE, LANES)
                total = jnp.zeros((TILE, LANES), jnp.float32)
                for p in range(planes):
                    total = jnp.where(plane == p, found[p], total)
                obs_ref[0, y, b] = total.astype(jnp.bfloat16)
        return 0

    lax.fori_loop(0, rows // pace, observe, 0)


def stencil(flags, turned, first, second, coef, smalls, held, tile, local, splits, fields, rows, levels, cols):
    planes = fields * levels
    blocks = len(smalls)
    tiles = coef.shape[0] // TILE
    outs = [jax.ShapeDtypeStruct((count, cols // LANES, rows * TILE, LANES), jnp.bfloat16) for _, count in splits]
    observed = jax.ShapeDtypeStruct((tiles, rows, blocks, TILE, LANES), jnp.bfloat16)
    room = pltpu.VMEM((planes, rows + 2 * STEPS, TILE, cols), jnp.float32)
    far = pl.BlockSpec(memory_space=pltpu.HBM)

    near = pl.BlockSpec(memory_space=pltpu.VMEM)
    in_specs = [pl.BlockSpec(memory_space=pltpu.SMEM), far, near, near, pl.BlockSpec((TILE, fields), lambda i: (tile, 0))]
    in_specs += [near] * len(smalls)
    args = [flags, pltpu.with_memory_space_constraint(turned, pltpu.HBM), first, second, coef, *(near_core(small) for small in smalls)]
    aliases = {}
    if held is not None:
        aliases = {len(args): len(splits)}
        in_specs.append(far)
        args.append(held)
    return pl.pallas_call(
        lambda *refs: stencil_kernel(fields, rows, levels, cols, blocks, splits, local, len(aliases), *refs),
        grid=(1,),
        in_specs=in_specs,
        out_specs=[pl.BlockSpec(out.shape, lambda i: (0, 0, 0, 0)) for out in outs]
        + [pl.BlockSpec((1, *observed.shape[1:]), lambda i: (tile, 0, 0, 0, 0))],
        out_shape=[*outs, observed],
        scratch_shapes=[
            room,
            room,
            pltpu.VMEM((planes, rows, TILE, cols), jnp.float32),
            pltpu.SemaphoreType.DMA,
        ],
        input_output_aliases=aliases,
        compiler_params=pltpu.CompilerParams(vmem_limit_bytes=KERNEL_VMEM),
        name="stencil",
    )(*args)


def product(a, b):
    a_high = a.astype(jnp.bfloat16)
    a_low = (a - a_high.astype(jnp.float32)).astype(jnp.bfloat16)
    b_high = b.astype(jnp.bfloat16)
    b_low = (b - b_high.astype(jnp.float32)).astype(jnp.bfloat16)
    left = jnp.concatenate([a_high, a_low], axis=1)
    right = jnp.concatenate(
        [jnp.concatenate([b_high, b_low], axis=1), jnp.concatenate([b_high, jnp.zeros_like(b_low)], axis=1)], axis=0
    )
    both = jnp.dot(left, right, preferred_element_type=jnp.float32)
    return both[:, :b.shape[1]] + both[:, b.shape[1]:]


def solve_kernel(rows, members, ensemble, pairs, flags_ref, table_ref, own_ref, near_ref, far_ref, upper_ref, lower_ref, sum_ref, wide, ys, zs, ms, gs, scales, direct):
    width = 2 * ensemble
    count = rows * pairs
    odd = flags_ref[ODD] == 1

    def fill(r, _):
        for q in range(pairs):
            near = near_ref[r, q].astype(jnp.float32)
            far = far_ref[r, q].astype(jnp.float32)
            wide[r, q] = jnp.where(odd, near, far)
            wide[rows + r, q] = own_ref[r, q]
            wide[2 * rows + r, q] = jnp.where(odd, far, near)
        return 0

    lax.fori_loop(0, rows, fill, 0)

    lane = lax.broadcasted_iota(jnp.int32, (ensemble, width), 1)
    first = lane < ensemble
    eye = jnp.where(
        lax.broadcasted_iota(jnp.int32, (width, width), 0) == lax.broadcasted_iota(jnp.int32, (width, width), 1), 1.0, 0.0
    )
    first_row = lax.broadcasted_iota(jnp.int32, (TILE, width), 1) < ensemble

    def localize(y, _):
        for q in range(pairs):
            local = jnp.zeros(wide.shape[2:], jnp.float32)
            for d in range(-HALO, HALO + 1):
                local = local + table_ref[d + HALO, y] * wide[rows + y + d, q]
            gram = local[:ensemble]
            amat = jnp.concatenate([jnp.where(first, gram, 0.0), jnp.where(first, 0.0, gram)], axis=0) + (ensemble - 1.0) * eye
            square = amat * amat
            tops = jnp.sqrt(jnp.sum(square[:ensemble], axis=(0, 1), keepdims=True))
            ends = jnp.sqrt(jnp.sum(square[ensemble:], axis=(0, 1), keepdims=True))
            part = jnp.concatenate(
                [jnp.broadcast_to(1.0 / tops, (ensemble, width)), jnp.broadcast_to(1.0 / ends, (ensemble, width))], axis=0
            )
            at = y * pairs + q
            ys[at] = amat * part
            gs[at] = local[ensemble:ensemble + TILE]
            scales[at] = jnp.where(first_row, tops, ends)
        return 0

    lax.fori_loop(0, rows, localize, 0)

    pace = 4 if count % 4 == 0 else 1

    def each(work):
        def some(i, _):
            for k in range(pace):
                work(pace * i + k)
            return 0

        lax.fori_loop(0, count // pace, some, 0)

    for step_idx in range(NS_STEPS):
        def middle(i):
            ms[i] = 1.5 * eye - 0.5 * (product(zs[i], ys[i]) if step_idx else ys[i])

        def apply(i):
            if step_idx < NS_STEPS - 1:
                ys[i] = product(ys[i], ms[i])
            zs[i] = product(ms[i], zs[i]) if step_idx else ms[i]

        each(middle)
        each(apply)

    def weigh(y, total):
        for q in range(pairs):
            at = y * pairs + q
            z, scale = zs[at], scales[at]
            mean = (product(product(gs[at], z), z) / scale)[:1]
            wpert = z[:members] + z[ensemble:ensemble + members]
            weights = wpert * (math.sqrt(ensemble - 1.0) / jnp.sqrt(scale))[:1] + mean
            total = total + weights
            here = first[:members]
            low = jnp.sum(jnp.where(here, weights, 0.0), axis=1, keepdims=True)
            high = jnp.sum(jnp.where(here, 0.0, weights), axis=1, keepdims=True)
            direct[q, pl.ds(y, members, stride=rows), :] = weights + (1.0 - jnp.where(here, low, high)) / ensemble
        return total

    sum_ref[...] = lax.fori_loop(0, rows, weigh, jnp.zeros((members, width), jnp.float32))

    depth = ensemble * rows
    column = lax.broadcasted_iota(jnp.int32, (width, depth), 1)
    member = column // (rows * TILE) * TILE + column % TILE
    entry = lax.broadcasted_iota(jnp.int32, (width, depth), 0)
    mine = lax.broadcasted_iota(jnp.int32, (members * rows, depth), 0) % rows
    theirs = lax.broadcasted_iota(jnp.int32, (members * rows, depth), 1) // TILE % rows
    keep = mine == theirs
    for half in range(2):
        place = jnp.where(entry == member + half * ensemble, 1.0, 0.0).astype(jnp.bfloat16)
        for q in range(pairs):
            w = direct[q]
            high = w.astype(jnp.bfloat16)
            low = (w - high.astype(jnp.float32)).astype(jnp.bfloat16)
            for part, ref in ((high, upper_ref), (low, lower_ref)):
                spread = jnp.dot(part, place, preferred_element_type=jnp.float32)
                ref[2 * q + half] = jnp.where(keep, spread, 0.0).astype(jnp.bfloat16)


def solve(flags, table, own, near, far, members, ensemble):
    rows, pairs, tall, width = own.shape
    count = rows * pairs
    out = pltpu.VMEM((2 * pairs, members * rows, ensemble * rows), jnp.bfloat16)
    square = pltpu.VMEM((count, width, width), jnp.float32)
    line = pltpu.VMEM((count, TILE, width), jnp.float32)
    smem = pl.BlockSpec(memory_space=pltpu.SMEM)
    vmem = pl.BlockSpec(memory_space=pltpu.VMEM)
    return pl.pallas_call(
        lambda *refs: solve_kernel(rows, members, ensemble, pairs, *refs),
        in_specs=[smem, smem, vmem, vmem, vmem],
        out_specs=[vmem] * 3,
        out_shape=[out, out, jax.ShapeDtypeStruct((members, width), jnp.float32)],
        scratch_shapes=[
            pltpu.VMEM((3 * rows, pairs, tall, width), jnp.float32),
            square, square, square, line, line,
            pltpu.VMEM((pairs, members * rows, width), jnp.float32),
        ],
        compiler_params=pltpu.CompilerParams(vmem_limit_bytes=KERNEL_VMEM),
        name="solve",
    )(flags, table, own, near, far)


def update_kernel(members, rows, cols, blocks, offsets, flags_ref, upper, lower, *rest):
    pieces, out_ref = rest[:len(offsets)], rest[-1]
    plane = pl.program_id(0)
    groups = cols // blocks // LANES
    for b in range(blocks):
        columns = []
        for s in range(b * groups, (b + 1) * groups):
            columns.append(jnp.concatenate([piece[at + plane, s] for piece, at in zip(pieces, offsets)], axis=0))
        x = jnp.concatenate(columns, axis=1) if groups > 1 else columns[0]
        mine = (b + blocks - flags_ref[ME]) % blocks
        total = jnp.dot(upper[mine], x, preferred_element_type=jnp.float32)
        total = total + jnp.dot(lower[mine], x, preferred_element_type=jnp.float32)
        total = total.reshape(members, rows, groups * LANES).astype(jnp.bfloat16)
        out_ref[:, 0, :, b * groups * LANES:(b + 1) * groups * LANES] = total


def update(flags, upper, lower, pieces, offsets, start, count, held, members, planes, rows, cols):
    blocks = upper.shape[0]
    in_specs = [pl.BlockSpec(memory_space=pltpu.SMEM)]
    in_specs += [pl.BlockSpec(memory_space=pltpu.VMEM)] * (2 + len(pieces))
    args = [flags, upper, lower, *(near_core(piece) for piece in pieces)]
    aliases = {}
    if held is not None:
        aliases = {len(args): 0}
        in_specs.append(pl.BlockSpec(memory_space=pl.ANY))
        args.append(held)
    return pl.pallas_call(
        lambda *refs: update_kernel(members, rows, cols, blocks, offsets, *refs),
        grid=(count,),
        in_specs=in_specs,
        out_specs=pl.BlockSpec((members, 1, rows, cols), lambda i: (0, start + i, 0, 0)),
        out_shape=jax.ShapeDtypeStruct((members, planes, rows, cols), jnp.bfloat16),
        input_output_aliases=aliases,
        compiler_params=pltpu.CompilerParams(vmem_limit_bytes=KERNEL_VMEM),
        name="update",
    )(*args)


def near_core(array):
    return pltpu.with_memory_space_constraint(array, pltpu.VMEM)


def from_member(array, shift):
    count = lax.axis_size("member")
    return lax.ppermute(array, "member", [((i + shift) % count, i) for i in range(count)])


def all_members(array):
    return [array] + [from_member(array, shift) for shift in range(1, lax.axis_size("member"))]


def swap_one(array):
    return lax.ppermute(array, "slab", [(i, i ^ 1) for i in range(lax.axis_size("slab"))])


def swap_two(array):
    pairs = [(i, i + 1) for i in range(1, lax.axis_size("slab") - 1, 2)]
    return lax.ppermute(array, "slab", pairs + [(j, i) for i, j in pairs])


def groups_of(planes):
    sizes = [2] * (planes // 2 - 1) + [1, 1] if planes % 2 == 0 else [1] * planes
    return [(sum(sizes[:i]), size) for i, size in enumerate(sizes)]


def cycle(prior_ensemble_fields, params, influence, obs_cell, obs_value, obs_prec, cutoff):
    highest = lax.Precision.HIGHEST
    fine_grain = lax.Precision.HIGH
    members, fields, rows, levels, cols = prior_ensemble_fields.shape
    planes = fields * levels
    tiles = members // TILE
    devices = lax.axis_size("member")
    slabs = lax.axis_size("slab")
    ensemble = members * devices
    me = lax.axis_index("member")
    place = lax.axis_index("slab")
    dims = (fields, rows, levels, cols)
    x2 = prior_ensemble_fields.reshape(members * fields * rows * levels * (cols // LANES), LANES)

    flags = jnp.stack([place % 2, me, place > 0, place < slabs - 1]).astype(jnp.int32)

    *packed, turned = pack(flags, x2, 0, 1, *dims)
    turned = [(turned, 0)]
    if tiles > 1:
        *more, others = pack(flags, x2, 1, tiles - 1, *dims)
        packed += more
        turned += [(others, i) for i in range(tiles - 1)]
    edges = []
    for i in range(tiles):
        edges.append((near_core(swap_one(packed[2 * i])), near_core(swap_two(packed[2 * i + 1]))))

    columns = obs_cell.shape[2]
    npar = params.shape[1]
    own_small = jnp.concatenate(
        [obs_cell[:, 0].astype(jnp.float32), obs_value[:, 0], obs_prec[:, 0]]
        + [jnp.pad(params.T, ((0, -npar % TILE), (0, columns - members)))]
    )
    smalls = all_members(own_small)
    every_param = jnp.concatenate([small[3 * rows:3 * rows + npar, :members].T for small in smalls])
    values = jnp.stack([small[rows:2 * rows] for small in smalls], axis=1)
    precs = jnp.stack([small[2 * rows:3 * rows] for small in smalls], axis=1)

    coef = jnp.dot(params, influence.astype(jnp.float32), precision=highest)

    fine = groups_of(planes)
    forecasts, own_obs = [], None
    for i in range(tiles):
        splits = fine if i == tiles - 1 else [(0, planes)]
        fields_here, local = turned[i]
        *outs, own_obs = stencil(flags, fields_here, *edges[i], coef, smalls, own_obs, i, local, splits, *dims)
        forecasts.append(outs)
    ens_obs = jnp.stack([jnp.roll(array, shift, axis=2) for shift, array in enumerate(all_members(own_obs))])
    sent = []
    for outs in forecasts:
        arrays = []
        for out in outs:
            arrays.append(all_members(out))
        sent.append(arrays)

    ens_obs = ens_obs.transpose(2, 3, 0, 1, 4, 5).reshape(rows, devices, ensemble, LANES).astype(jnp.float32)
    ybar = jnp.mean(ens_obs, axis=2, keepdims=True)
    ypert = ens_obs - ybar
    weighted = precs * (values - ybar[:, :, 0])
    gram = jnp.einsum("rbeo,rbfo->rbef", ypert * precs[:, :, None], ypert, precision=fine_grain)
    gvec = jnp.einsum("rbeo,rbo->rbe", ypert, weighted, precision=highest)
    empty = jnp.zeros((rows, devices, TILE - 1, ensemble), jnp.float32)
    stacked = jnp.concatenate([gram, gvec[:, :, None, :], empty], axis=2)
    stacked = jnp.concatenate([stacked[:, 0::2], stacked[:, 1::2]], axis=3)
    rounded = stacked.astype(jnp.bfloat16)
    near, far = near_core(swap_one(rounded)), near_core(swap_two(rounded))
    radius = cutoff.astype(jnp.float32)
    distance = jnp.abs(jnp.arange(-HALO, HALO + 1, dtype=jnp.float32))[:, None]
    table = jnp.maximum(0.0, 1.0 - distance / (radius + 1.0))
    upper, lower, weight_rows = solve(flags, table, near_core(stacked), near, far, members, ensemble)

    analysis = None
    for g, (start, count) in enumerate(fine):
        pieces, offsets = [], []
        for r in range(devices):
            for arrays in sent:
                pieces.append(arrays[g if len(arrays) > 1 else 0][r])
                offsets.append(0 if len(arrays) > 1 else start)
        analysis = update(flags, upper, lower, pieces, offsets, start, count, analysis, members, planes, rows, cols)
    analysis = analysis.reshape(members, fields, levels, rows, cols).transpose(0, 1, 3, 2, 4)

    pbar = jnp.mean(every_param, axis=0)
    ppert = every_param - pbar
    weight_rows = weight_rows[:, :ensemble] + weight_rows[:, ensemble:]
    part = jnp.einsum("jk,ej->ke", ppert, weight_rows, precision=highest)
    step = 1
    while step < slabs:
        part = part + lax.ppermute(part, "slab", [(i, i ^ step) for i in range(slabs)])
        step *= 2
    total = part / (rows * slabs * devices)
    param_analysis = pbar + total.T
    return (analysis, param_analysis)


def solution(mesh):
    in_specs = (
        P("member", None, "slab", None, None),
        P("member", None),
        P(),
        P("slab", "member", None),
        P("slab", "member", None),
        P("slab", "member", None),
        P("slab"),
    )
    out_specs = (P("member", None, "slab", None, None), P("member", None))
    return jax.shard_map(cycle, mesh=mesh, in_specs=in_specs, out_specs=out_specs, check_vma=False)
```

```python
import math

import jax
import jax.numpy as jnp
from jax import lax
from jax.experimental import pallas as pl
from jax.experimental.pallas import tpu as pltpu
from jax.sharding import PartitionSpec as P


HALO = 8
STEPS = 4
NS_STEPS = 5
LANES = 128
TILE = 8
PACE = 4
HEAD = 1
KERNEL_VMEM = 44 * 1024 * 1024

diffusion = 0.2
advection = 0.15
vertical = 0.1
coupling = 0.2


def planes_of(fields, levels):
    return [(f, l) for f in range(fields) for l in range(levels)]


def place_in_pair():
    return lax.axis_index("slab") % 2


def pack_kernel(fields, rows, levels, cols, count, keep, x_ref, *rest):
    outs, edges, sems = rest[:2 * count + 1], *rest[2 * count + 1:2 * count + 3]
    turned = outs[-1] if keep else rest[-1]
    groups = cols // LANES
    stride = fields * rows * levels * groups
    planes = fields * levels
    tile = pl.program_id(0)

    def row(y, _):
        for p, (f, l) in enumerate(planes_of(fields, levels)):
            for s in range(groups):
                start = ((f * rows + y) * levels + l) * groups + s
                turned[tile, p, y, :, s * LANES:(s + 1) * LANES] = x_ref[pl.ds(start, TILE, stride=stride), :]
        return 0

    lax.fori_loop(0, rows, row, 0)

    def edge(y, _):
        for side in range(2):
            at = jnp.where(place_in_pair() == side, rows - STEPS, 0) + y
            for p in range(planes):
                edges[tile, side, p, y] = turned[tile, p, at].astype(jnp.bfloat16)
        return 0

    lax.fori_loop(0, STEPS, edge, 0)

    def copies(k):
        pairs = [(edges.at[k, 0], outs[2 * k]), (edges.at[k, 1], outs[2 * k + 1])]
        if not keep:
            pairs.append((turned.at[k], outs[-1].at[k]))
        return [pltpu.make_async_copy(src, dst, sems.at[k, i]) for i, (src, dst) in enumerate(pairs)]

    for k in range(count):
        @pl.when(tile == k)
        def _():
            for copy in copies(k):
                copy.start()

    @pl.when(tile == count - 1)
    def _():
        for k in range(count):
            for copy in copies(k):
                copy.wait()


def pack(x2, first, count, keep, fields, rows, levels, cols):
    limit = {"vmem_limit_bytes": KERNEL_VMEM} if keep else {}
    planes = fields * levels
    block = TILE * fields * rows * levels * cols // LANES
    edge = (planes, STEPS, TILE, cols)
    turned = (count, planes, rows, TILE, cols)
    return pl.pallas_call(
        lambda *refs: pack_kernel(fields, rows, levels, cols, count, keep, *refs),
        grid=(count,),
        in_specs=[pl.BlockSpec((block, LANES), lambda i: (first + i, 0))],
        out_specs=[pl.BlockSpec(memory_space=pltpu.HBM)] * (2 * count)
        + [pl.BlockSpec(memory_space=pltpu.VMEM if keep else pltpu.HBM)],
        out_shape=[jax.ShapeDtypeStruct(edge, jnp.bfloat16)] * (2 * count)
        + [pltpu.VMEM(turned, jnp.float32) if keep else jax.ShapeDtypeStruct(turned, jnp.float32)],
        scratch_shapes=[
            pltpu.VMEM((count, 2, *edge), jnp.bfloat16),
            pltpu.SemaphoreType.DMA((count, 3)),
        ]
        + ([] if keep else [pltpu.VMEM(turned, jnp.float32)]),
        compiler_params=pltpu.CompilerParams(**limit),
        name="pack",
    )(pltpu.with_memory_space_constraint(x2, pltpu.HBM))


def stencil_kernel(fields, rows, levels, cols, blocks, splits, local, held, x_ref, first_ref, second_ref, coef_ref, *rest):
    small_refs, rest = rest[:blocks], rest[blocks + held:]
    out_refs = rest[:len(splits)]
    obs_ref = rest[len(splits)]
    *state, mixed, sem = rest[len(splits) + 1:]
    groups = cols // LANES
    block_cols = cols // blocks
    pairs = planes_of(fields, levels)
    planes = len(pairs)

    own_copy = pltpu.make_async_copy(x_ref.at[local], state[0].at[:, pl.ds(STEPS, rows)], sem)
    own_copy.start()

    def tile_at(s):
        return slice(s * LANES, (s + 1) * LANES)

    odd = place_in_pair() == 1

    def load_edge(y, _):
        for p in range(planes):
            first = first_ref[p, y].astype(jnp.float32)
            second = second_ref[p, y].astype(jnp.float32)
            state[0][p, y] = jnp.where(odd, first, second)
            state[0][p, STEPS + rows + y] = jnp.where(odd, second, first)
        return 0

    lax.fori_loop(0, STEPS, load_edge, 0)
    own_copy.wait()
    place = lax.axis_index("slab")
    is_open = [jnp.where(place > 0, 1.0, 0.0), jnp.where(place < lax.axis_size("slab") - 1, 1.0, 0.0)]

    lane = lax.broadcasted_iota(jnp.int32, (TILE, LANES), 1)
    at_last = lane == LANES - 1
    at_first = lane == 0
    centre = (1.0 - 4.0 * diffusion - vertical) / diffusion
    below_part = vertical / diffusion
    right_part = (diffusion - advection) / diffusion
    left_part = (diffusion + advection) / diffusion
    next_part = coupling / diffusion
    scale = diffusion ** STEPS
    coefs = [jnp.broadcast_to(next_part * coef_ref[:, f:f + 1], (TILE, LANES)) for f in range(fields)]

    def rest_of_step(src, y, p):
        f, l = pairs[p]
        after = ((f + 1) % fields) * levels + l
        under = f * levels + (l - 1) % levels
        mid, out = [], []
        for s in range(groups):
            here = src[p, y, :, tile_at(s)]
            around = src[p, y + 1, :, tile_at(s)] + src[p, y - 1, :, tile_at(s)]
            if under == p:
                whole = centre + below_part
                own = here if abs(whole - 1.0) < 1e-12 else whole * here
            else:
                own = centre * here + below_part * src[under, y, :, tile_at(s)]
            mid.append(here)
            out.append((around + own) + coefs[f] * src[after, y, :, tile_at(s)])
        return mid, out

    def shifted(tiles):
        moved = []
        for s in range(0, groups, 2):
            both = jnp.concatenate(tiles[s:s + 2], axis=0).astype(jnp.bfloat16)
            both = pltpu.roll(both, LANES - 1, 1).astype(jnp.float32)
            moved += [both[k:k + TILE] for k in range(0, both.shape[0], TILE)]
        return moved

    pace = PACE if rows % PACE == 0 else 1
    for t in range(1, STEPS + 1):
        src, dst = state[(t - 1) % 2], state[t % 2]
        reach = STEPS - t
        ratio = math.comb(STEPS, t - 1) / math.comb(STEPS, t)

        def edge_rows(i, _):
            for side, y in enumerate((t + i, STEPS + rows + i)):
                for p in range(planes):
                    for s, value in enumerate(rest_of_step(src, y, p)[1]):
                        dst[p, y, :, tile_at(s)] = value * is_open[side]
            return 0

        def own_rows(i, _):
            for k in range(pace):
                mine = pace * i + k
                for p in range(planes):
                    mid, out = rest_of_step(src, STEPS + mine, p)
                    if t > 1:
                        mid = [mixed[p, mine, :, tile_at(s)] for s in range(groups)]
                    ahead = shifted(mid)
                    behind = [pltpu.roll(v, 1, 1) for v in mid]
                    for s in range(groups):
                        right = jnp.where(at_last, ahead[(s + 1) % groups], ahead[s])
                        left = jnp.where(at_first, behind[(s - 1) % groups], behind[s])
                        value = out[s] + (ratio * right_part * right + ratio * left_part * left)
                        if t < STEPS:
                            dst[p, STEPS + mine, :, tile_at(s)] = out[s]
                            mixed[p, mine, :, tile_at(s)] = value
                            continue
                        value = value * scale
                        mixed[p, mine, :, tile_at(s)] = value
                        for g, (start, count) in enumerate(splits):
                            if start <= p < start + count:
                                at = pl.ds(pl.multiple_of(mine * TILE, TILE), TILE)
                                out_refs[g][p - start, s, at, :] = value.astype(jnp.bfloat16)
            return 0

        if reach:
            lax.fori_loop(0, reach, edge_rows, 0)
        lax.fori_loop(0, rows // pace, own_rows, 0)

    column = lax.broadcasted_iota(jnp.int32, (block_cols, LANES), 0)

    def observe(i, _):
        for k in range(pace):
            y = pace * i + k
            for b in range(blocks):
                cell = small_refs[b][pl.ds(y, 1), :].astype(jnp.int32)
                plane = cell // block_cols
                pick = jnp.where(column == cell - plane * block_cols, 1.0, 0.0).astype(jnp.bfloat16)
                start = (lax.axis_index("member") + b) % blocks * block_cols
                part = mixed[:, y, :, pl.ds(pl.multiple_of(start, LANES), block_cols)]
                part = part.reshape(planes * TILE, block_cols).astype(jnp.bfloat16)
                found = jnp.dot(part, pick, preferred_element_type=jnp.float32).reshape(planes, TILE, LANES)
                total = jnp.zeros((TILE, LANES), jnp.float32)
                for p in range(planes):
                    total = jnp.where(plane == p, found[p], total)
                obs_ref[0, y, b] = total.astype(jnp.bfloat16)
        return 0

    lax.fori_loop(0, rows // pace, observe, 0)


def stencil(turned, first, second, coef, smalls, held, tile, local, splits, fields, rows, levels, cols):
    planes = fields * levels
    blocks = len(smalls)
    tiles = coef.shape[0] // TILE
    outs = [jax.ShapeDtypeStruct((count, cols // LANES, rows * TILE, LANES), jnp.bfloat16) for _, count in splits]
    observed = jax.ShapeDtypeStruct((tiles, rows, blocks, TILE, LANES), jnp.bfloat16)
    room = pltpu.VMEM((planes, rows + 2 * STEPS, TILE, cols), jnp.float32)
    far = pl.BlockSpec(memory_space=pltpu.HBM)

    near = pl.BlockSpec(memory_space=pltpu.VMEM)
    in_specs = [near if tile < HEAD else far, near, near, pl.BlockSpec((TILE, fields), lambda i: (tile, 0))]
    in_specs += [near] * len(smalls)
    args = [turned, first, second, coef, *(near_core(small) for small in smalls)]
    aliases = {}
    if held is not None:
        aliases = {len(args): len(splits)}
        in_specs.append(far)
        args.append(held)
    return pl.pallas_call(
        lambda *refs: stencil_kernel(fields, rows, levels, cols, blocks, splits, local, len(aliases), *refs),
        grid=(1,),
        in_specs=in_specs,
        out_specs=[pl.BlockSpec(out.shape, lambda i: (0, 0, 0, 0)) for out in outs]
        + [pl.BlockSpec((1, *observed.shape[1:]), lambda i: (tile, 0, 0, 0, 0))],
        out_shape=[*outs, observed],
        scratch_shapes=[
            room,
            room,
            pltpu.VMEM((planes, rows, TILE, cols), jnp.float32),
            pltpu.SemaphoreType.DMA,
        ],
        input_output_aliases=aliases,
        compiler_params=pltpu.CompilerParams(vmem_limit_bytes=KERNEL_VMEM),
        name="stencil",
    )(*args)


def product(a, b):
    a_high = a.astype(jnp.bfloat16)
    a_low = (a - a_high.astype(jnp.float32)).astype(jnp.bfloat16)
    b_high = b.astype(jnp.bfloat16)
    b_low = (b - b_high.astype(jnp.float32)).astype(jnp.bfloat16)
    left = jnp.concatenate([a_high, a_low], axis=1)
    right = jnp.concatenate(
        [jnp.concatenate([b_high, b_low], axis=1), jnp.concatenate([b_high, jnp.zeros_like(b_low)], axis=1)], axis=0
    )
    both = jnp.dot(left, right, preferred_element_type=jnp.float32)
    return both[:, :b.shape[1]] + both[:, b.shape[1]:]


def solve_kernel(rows, members, ensemble, pairs, table_ref, own_ref, near_ref, far_ref, upper_ref, lower_ref, sum_ref, wide, ys, zs, ms, gs, scales, direct):
    width = 2 * ensemble
    count = rows * pairs
    odd = place_in_pair() == 1

    def fill(r, _):
        for q in range(pairs):
            near = near_ref[r, q].astype(jnp.float32)
            far = far_ref[r, q].astype(jnp.float32)
            wide[r, q] = jnp.where(odd, near, far)
            wide[rows + r, q] = own_ref[r, q]
            wide[2 * rows + r, q] = jnp.where(odd, far, near)
        return 0

    lax.fori_loop(0, rows, fill, 0)

    lane = lax.broadcasted_iota(jnp.int32, (ensemble, width), 1)
    first = lane < ensemble
    eye = jnp.where(
        lax.broadcasted_iota(jnp.int32, (width, width), 0) == lax.broadcasted_iota(jnp.int32, (width, width), 1), 1.0, 0.0
    )
    first_row = lax.broadcasted_iota(jnp.int32, (TILE, width), 1) < ensemble

    def localize(i, _):
        for y, q in ((2 * i + k, q) for k in range(2) for q in range(pairs)):
            local = jnp.zeros(wide.shape[2:], jnp.float32)
            for d in range(-HALO, HALO + 1):
                local = local + table_ref[d + HALO, y] * wide[rows + y + d, q]
            gram = local[:ensemble]
            amat = jnp.concatenate([jnp.where(first, gram, 0.0), jnp.where(first, 0.0, gram)], axis=0) + (ensemble - 1.0) * eye
            square = amat * amat
            tops = jnp.sqrt(jnp.sum(square[:ensemble], axis=(0, 1), keepdims=True))
            ends = jnp.sqrt(jnp.sum(square[ensemble:], axis=(0, 1), keepdims=True))
            part = jnp.concatenate(
                [jnp.broadcast_to(1.0 / tops, (ensemble, width)), jnp.broadcast_to(1.0 / ends, (ensemble, width))], axis=0
            )
            at = y * pairs + q
            ys[at] = amat * part
            gs[at] = local[ensemble:ensemble + TILE]
            scales[at] = jnp.where(first_row, tops, ends)
        return 0

    lax.fori_loop(0, rows // 2, localize, 0)

    pace = 8 if count % 8 == 0 else 1

    def each(work):
        def some(i, _):
            for k in range(pace):
                work(pace * i + k)
            return 0

        lax.fori_loop(0, count // pace, some, 0)

    for step_idx in range(NS_STEPS):
        def middle(i):
            ms[i] = 1.5 * eye - 0.5 * (product(zs[i], ys[i]) if step_idx else ys[i])

        def apply(i):
            if step_idx < NS_STEPS - 1:
                ys[i] = product(ys[i], ms[i])
            zs[i] = product(ms[i], zs[i]) if step_idx else ms[i]

        each(middle)
        each(apply)

    def weigh(i, total):
        for y, q in ((2 * i + k, q) for k in range(2) for q in range(pairs)):
            at = y * pairs + q
            z, scale = zs[at], scales[at]
            mean = (product(product(gs[at], z), z) / scale)[:1]
            wpert = z[:members] + z[ensemble:ensemble + members]
            weights = wpert * (math.sqrt(ensemble - 1.0) / jnp.sqrt(scale))[:1] + mean
            total = total + weights
            here = first[:members]
            low = jnp.sum(jnp.where(here, weights, 0.0), axis=1, keepdims=True)
            high = jnp.sum(jnp.where(here, 0.0, weights), axis=1, keepdims=True)
            direct[q, pl.ds(y, members, stride=rows), :] = weights + (1.0 - jnp.where(here, low, high)) / ensemble
        return total

    sum_ref[...] = lax.fori_loop(0, rows // 2, weigh, jnp.zeros((members, width), jnp.float32))

    depth = ensemble * rows
    column = lax.broadcasted_iota(jnp.int32, (width, depth), 1)
    member = column // (rows * TILE) * TILE + column % TILE
    entry = lax.broadcasted_iota(jnp.int32, (width, depth), 0)
    mine = lax.broadcasted_iota(jnp.int32, (members * rows, depth), 0) % rows
    theirs = lax.broadcasted_iota(jnp.int32, (members * rows, depth), 1) // TILE % rows
    keep = mine == theirs
    for half in range(2):
        place = jnp.where(entry == member + half * ensemble, 1.0, 0.0).astype(jnp.bfloat16)
        for q in range(pairs):
            w = direct[q]
            high = w.astype(jnp.bfloat16)
            low = (w - high.astype(jnp.float32)).astype(jnp.bfloat16)
            for part, ref in ((high, upper_ref), (low, lower_ref)):
                spread = jnp.dot(part, place, preferred_element_type=jnp.float32)
                ref[2 * q + half] = jnp.where(keep, spread, 0.0).astype(jnp.bfloat16)


def solve(table, own, near, far, members, ensemble):
    rows, pairs, tall, width = own.shape
    count = rows * pairs
    out = pltpu.VMEM((2 * pairs, members * rows, ensemble * rows), jnp.bfloat16)
    square = pltpu.VMEM((count, width, width), jnp.float32)
    line = pltpu.VMEM((count, TILE, width), jnp.float32)
    smem = pl.BlockSpec(memory_space=pltpu.SMEM)
    vmem = pl.BlockSpec(memory_space=pltpu.VMEM)
    return pl.pallas_call(
        lambda *refs: solve_kernel(rows, members, ensemble, pairs, *refs),
        in_specs=[smem, vmem, vmem, vmem],
        out_specs=[vmem] * 3,
        out_shape=[out, out, jax.ShapeDtypeStruct((members, width), jnp.float32)],
        scratch_shapes=[
            pltpu.VMEM((3 * rows, pairs, tall, width), jnp.float32),
            square, square, square, line, line,
            pltpu.VMEM((pairs, members * rows, width), jnp.float32),
        ],
        compiler_params=pltpu.CompilerParams(vmem_limit_bytes=KERNEL_VMEM),
        name="solve",
    )(table, own, near, far)


def update_kernel(members, rows, cols, blocks, offsets, upper, lower, *rest):
    pieces, out_ref = rest[:len(offsets)], rest[-1]
    plane, b = pl.program_id(0), pl.program_id(1)
    groups = cols // blocks // LANES
    columns = []
    for s in range(groups):
        columns.append(jnp.concatenate([piece[at + plane, b * groups + s] for piece, at in zip(pieces, offsets)], axis=0))
    x = jnp.concatenate(columns, axis=1) if groups > 1 else columns[0]
    mine = (b + blocks - lax.axis_index("member")) % blocks
    total = jnp.dot(upper[mine], x, preferred_element_type=jnp.float32)
    total = total + jnp.dot(lower[mine], x, preferred_element_type=jnp.float32)
    out_ref[:, 0] = total.reshape(members, rows, groups * LANES).astype(jnp.bfloat16)


def update(upper, lower, pieces, offsets, start, count, held, members, planes, rows, cols):
    blocks = upper.shape[0]
    in_specs = [pl.BlockSpec(memory_space=pltpu.VMEM)] * (2 + len(pieces))
    args = [upper, lower, *(near_core(piece) for piece in pieces)]
    aliases = {}
    if held is not None:
        aliases = {len(args): 0}
        in_specs.append(pl.BlockSpec(memory_space=pl.ANY))
        args.append(held)
    return pl.pallas_call(
        lambda *refs: update_kernel(members, rows, cols, blocks, offsets, *refs),
        grid=(count, blocks),
        in_specs=in_specs,
        out_specs=pl.BlockSpec((members, 1, rows, cols // blocks), lambda i, b: (0, start + i, 0, b)),
        out_shape=jax.ShapeDtypeStruct((members, planes, rows, cols), jnp.bfloat16),
        input_output_aliases=aliases,
        compiler_params=pltpu.CompilerParams(vmem_limit_bytes=KERNEL_VMEM),
        name="update",
    )(*args)


def near_core(array):
    return pltpu.with_memory_space_constraint(array, pltpu.VMEM)


def from_member(array, shift):
    count = lax.axis_size("member")
    return lax.ppermute(array, "member", [((i + shift) % count, i) for i in range(count)])


def all_members(array):
    return [array] + [from_member(array, shift) for shift in range(1, lax.axis_size("member"))]


def swap_one(array):
    return lax.ppermute(array, "slab", [(i, i ^ 1) for i in range(lax.axis_size("slab"))])


def swap_two(array):
    pairs = [(i, i + 1) for i in range(1, lax.axis_size("slab") - 1, 2)]
    return lax.ppermute(array, "slab", pairs + [(j, i) for i, j in pairs])


def groups_of(planes):
    sizes = [2] * (planes // 2 - 1) + [1, 1] if planes % 2 == 0 else [1] * planes
    return [(sum(sizes[:i]), size) for i, size in enumerate(sizes)]


def cycle(prior_ensemble_fields, params, influence, obs_cell, obs_value, obs_prec, cutoff):
    highest = lax.Precision.HIGHEST
    fine_grain = lax.Precision.HIGH
    members, fields, rows, levels, cols = prior_ensemble_fields.shape
    planes = fields * levels
    tiles = members // TILE
    devices = lax.axis_size("member")
    slabs = lax.axis_size("slab")
    ensemble = members * devices
    dims = (fields, rows, levels, cols)
    x2 = prior_ensemble_fields.reshape(members * fields * rows * levels * (cols // LANES), LANES)

    head = min(HEAD, tiles)
    *packed, turned = pack(x2, 0, head, True, *dims)
    turned = [(turned, i) for i in range(head)]
    if tiles > head:
        *more, others = pack(x2, head, tiles - head, False, *dims)
        packed += more
        others = pltpu.with_memory_space_constraint(others, pltpu.HBM)
        turned += [(others, i) for i in range(tiles - head)]
    edges = []
    for i in range(tiles):
        edges.append((near_core(swap_one(packed[2 * i])), near_core(swap_two(packed[2 * i + 1]))))

    columns = obs_cell.shape[2]
    npar = params.shape[1]
    own_small = jnp.concatenate(
        [obs_cell[:, 0].astype(jnp.float32), obs_value[:, 0], obs_prec[:, 0]]
        + [jnp.pad(params.T, ((0, -npar % TILE), (0, columns - members)))]
    )
    smalls = all_members(own_small)
    every_param = jnp.concatenate([small[3 * rows:3 * rows + npar, :members].T for small in smalls])
    values = jnp.stack([small[rows:2 * rows] for small in smalls], axis=1)
    precs = jnp.stack([small[2 * rows:3 * rows] for small in smalls], axis=1)

    coef = jnp.dot(params, influence.astype(jnp.float32), precision=highest)

    fine = groups_of(planes)
    forecasts, own_obs = [], None
    for i in range(tiles):
        splits = [(0, planes)]
        if i == tiles - 1:
            splits = fine
        elif i == 1:
            splits = [(0, fine[-2][0]), (fine[-2][0], planes - fine[-2][0])]
        fields_here, local = turned[i]
        *outs, own_obs = stencil(fields_here, *edges[i], coef, smalls, own_obs, i, local, splits, *dims)
        forecasts.append((splits, outs))
    ens_obs = jnp.stack([jnp.roll(array, shift, axis=2) for shift, array in enumerate(all_members(own_obs))])
    sent = []
    for splits, outs in forecasts:
        arrays = []
        for out in outs:
            arrays.append(all_members(out))
        sent.append((splits, arrays))

    ens_obs = ens_obs.transpose(2, 3, 0, 1, 4, 5).reshape(rows, devices, ensemble, LANES).astype(jnp.float32)
    ybar = jnp.mean(ens_obs, axis=2, keepdims=True)
    ypert = ens_obs - ybar
    weighted = precs * (values - ybar[:, :, 0])
    gram = jnp.einsum("rbeo,rbfo->rbef", ypert * precs[:, :, None], ypert, precision=fine_grain)
    gvec = jnp.einsum("rbeo,rbo->rbe", ypert, weighted, precision=highest)
    empty = jnp.zeros((rows, devices, TILE - 1, ensemble), jnp.float32)
    stacked = jnp.concatenate([gram, gvec[:, :, None, :], empty], axis=2)
    stacked = jnp.concatenate([stacked[:, 0::2], stacked[:, 1::2]], axis=3)
    rounded = stacked.astype(jnp.bfloat16)
    near, far = near_core(swap_one(rounded)), near_core(swap_two(rounded))
    radius = cutoff.astype(jnp.float32)
    distance = jnp.abs(jnp.arange(-HALO, HALO + 1, dtype=jnp.float32))[:, None]
    table = jnp.maximum(0.0, 1.0 - distance / (radius + 1.0))
    upper, lower, weight_rows = solve(table, near_core(stacked), near, far, members, ensemble)

    analysis = None
    for start, count in fine:
        pieces, offsets = [], []
        for r in range(devices):
            for splits, arrays in sent:
                part = max(k for k, (at, _) in enumerate(splits) if at <= start)
                pieces.append(arrays[part][r])
                offsets.append(start - splits[part][0])
        analysis = update(upper, lower, pieces, offsets, start, count, analysis, members, planes, rows, cols)
    analysis = analysis.reshape(members, fields, levels, rows, cols).transpose(0, 1, 3, 2, 4)

    pbar = jnp.mean(every_param, axis=0)
    ppert = every_param - pbar
    weight_rows = weight_rows[:, :ensemble] + weight_rows[:, ensemble:]
    part = jnp.einsum("jk,ej->ke", ppert, weight_rows, precision=highest)
    step = 1
    while step < slabs:
        part = part + lax.ppermute(part, "slab", [(i, i ^ step) for i in range(slabs)])
        step *= 2
    total = part / (rows * slabs * devices)
    param_analysis = pbar + total.T
    return (analysis, param_analysis)


def solution(mesh):
    in_specs = (
        P("member", None, "slab", None, None),
        P("member", None),
        P(),
        P("slab", "member", None),
        P("slab", "member", None),
        P("slab", "member", None),
        P("slab"),
    )
    out_specs = (P("member", None, "slab", None, None), P("member", None))
    return jax.shard_map(cycle, mesh=mesh, in_specs=in_specs, out_specs=out_specs, check_vma=False)
```

```python
import math

import jax
import jax.numpy as jnp
from jax import lax
from jax.experimental import pallas as pl
from jax.experimental.pallas import tpu as pltpu
from jax.sharding import PartitionSpec as P


HALO = 8
STEPS = 4
NS_STEPS = 5
LANES = 128
TILE = 8
PACE = 4
HEAD = 1
KERNEL_VMEM = 44 * 1024 * 1024

diffusion = 0.2
advection = 0.15
vertical = 0.1
coupling = 0.2


def planes_of(fields, levels):
    return [(f, l) for f in range(fields) for l in range(levels)]


def place_in_pair():
    return lax.axis_index("slab") % 2


def pack_kernel(fields, rows, levels, cols, count, keep, x_ref, *rest):
    outs, edges, sems = rest[:2 * count + 1], *rest[2 * count + 1:2 * count + 3]
    turned = outs[-1] if keep else rest[-1]
    groups = cols // LANES
    stride = fields * rows * levels * groups
    planes = fields * levels
    tile = pl.program_id(0)

    def row(y, _):
        for p, (f, l) in enumerate(planes_of(fields, levels)):
            for s in range(groups):
                start = ((f * rows + y) * levels + l) * groups + s
                turned[tile, p, y, :, s * LANES:(s + 1) * LANES] = x_ref[pl.ds(start, TILE, stride=stride), :]
        return 0

    lax.fori_loop(0, rows, row, 0)

    def edge(y, _):
        for side in range(2):
            at = jnp.where(place_in_pair() == side, rows - STEPS, 0) + y
            for p in range(planes):
                edges[tile, side, p, y] = turned[tile, p, at].astype(jnp.bfloat16)
        return 0

    lax.fori_loop(0, STEPS, edge, 0)

    def copies(k):
        pairs = [(edges.at[k, 0], outs[2 * k]), (edges.at[k, 1], outs[2 * k + 1])]
        if not keep:
            pairs.append((turned.at[k], outs[-1].at[k]))
        return [pltpu.make_async_copy(src, dst, sems.at[k, i]) for i, (src, dst) in enumerate(pairs)]

    for k in range(count):
        @pl.when(tile == k)
        def _():
            for copy in copies(k):
                copy.start()

    @pl.when(tile == count - 1)
    def _():
        for k in range(count):
            for copy in copies(k):
                copy.wait()


def pack(x2, first, count, keep, fields, rows, levels, cols):
    limit = {"vmem_limit_bytes": KERNEL_VMEM} if keep else {}
    planes = fields * levels
    block = TILE * fields * rows * levels * cols // LANES
    edge = (planes, STEPS, TILE, cols)
    turned = (count, planes, rows, TILE, cols)
    return pl.pallas_call(
        lambda *refs: pack_kernel(fields, rows, levels, cols, count, keep, *refs),
        grid=(count,),
        in_specs=[pl.BlockSpec((block, LANES), lambda i: (first + i, 0))],
        out_specs=[pl.BlockSpec(memory_space=pltpu.HBM)] * (2 * count)
        + [pl.BlockSpec(memory_space=pltpu.VMEM if keep else pltpu.HBM)],
        out_shape=[jax.ShapeDtypeStruct(edge, jnp.bfloat16)] * (2 * count)
        + [pltpu.VMEM(turned, jnp.float32) if keep else jax.ShapeDtypeStruct(turned, jnp.float32)],
        scratch_shapes=[
            pltpu.VMEM((count, 2, *edge), jnp.bfloat16),
            pltpu.SemaphoreType.DMA((count, 3)),
        ]
        + ([] if keep else [pltpu.VMEM(turned, jnp.float32)]),
        compiler_params=pltpu.CompilerParams(**limit),
        name="pack",
    )(pltpu.with_memory_space_constraint(x2, pltpu.HBM))


def stencil_kernel(fields, rows, levels, cols, blocks, splits, local, held, x_ref, first_ref, second_ref, coef_ref, *rest):
    small_refs, rest = rest[:blocks], rest[blocks + held:]
    out_refs = rest[:len(splits)]
    obs_ref = rest[len(splits)]
    *state, mixed, sem = rest[len(splits) + 1:]
    groups = cols // LANES
    block_cols = cols // blocks
    pairs = planes_of(fields, levels)
    planes = len(pairs)

    own_copy = pltpu.make_async_copy(x_ref.at[local], state[0].at[:, pl.ds(STEPS, rows)], sem)
    own_copy.start()

    def tile_at(s):
        return slice(s * LANES, (s + 1) * LANES)

    odd = place_in_pair() == 1

    def load_edge(y, _):
        for p in range(planes):
            first = first_ref[p, y].astype(jnp.float32)
            second = second_ref[p, y].astype(jnp.float32)
            state[0][p, y] = jnp.where(odd, first, second)
            state[0][p, STEPS + rows + y] = jnp.where(odd, second, first)
        return 0

    lax.fori_loop(0, STEPS, load_edge, 0)
    own_copy.wait()
    place = lax.axis_index("slab")
    is_open = [jnp.where(place > 0, 1.0, 0.0), jnp.where(place < lax.axis_size("slab") - 1, 1.0, 0.0)]

    lane = lax.broadcasted_iota(jnp.int32, (TILE, LANES), 1)
    at_last = lane == LANES - 1
    at_first = lane == 0
    centre = (1.0 - 4.0 * diffusion - vertical) / diffusion
    below_part = vertical / diffusion
    right_part = (diffusion - advection) / diffusion
    left_part = (diffusion + advection) / diffusion
    next_part = coupling / diffusion
    scale = diffusion ** STEPS
    coefs = [jnp.broadcast_to(next_part * coef_ref[:, f:f + 1], (TILE, LANES)) for f in range(fields)]

    def rest_of_step(src, y, p):
        f, l = pairs[p]
        after = ((f + 1) % fields) * levels + l
        under = f * levels + (l - 1) % levels
        mid, out = [], []
        for s in range(groups):
            here = src[p, y, :, tile_at(s)]
            around = src[p, y + 1, :, tile_at(s)] + src[p, y - 1, :, tile_at(s)]
            if under == p:
                whole = centre + below_part
                own = here if abs(whole - 1.0) < 1e-12 else whole * here
            else:
                own = centre * here + below_part * src[under, y, :, tile_at(s)]
            mid.append(here)
            out.append((around + own) + coefs[f] * src[after, y, :, tile_at(s)])
        return mid, out

    def shifted(tiles):
        moved = []
        for s in range(0, groups, 2):
            both = jnp.concatenate(tiles[s:s + 2], axis=0).astype(jnp.bfloat16)
            both = pltpu.roll(both, LANES - 1, 1).astype(jnp.float32)
            moved += [both[k:k + TILE] for k in range(0, both.shape[0], TILE)]
        return moved

    pace = PACE if rows % PACE == 0 else 1
    for t in range(1, STEPS + 1):
        src, dst = state[(t - 1) % 2], state[t % 2]
        reach = STEPS - t
        ratio = math.comb(STEPS, t - 1) / math.comb(STEPS, t)

        def edge_rows(i, _):
            for side, y in enumerate((t + i, STEPS + rows + i)):
                for p in range(planes):
                    for s, value in enumerate(rest_of_step(src, y, p)[1]):
                        dst[p, y, :, tile_at(s)] = value * is_open[side]
            return 0

        def own_rows(i, _):
            for k in range(pace):
                mine = pace * i + k
                for p in range(planes):
                    mid, out = rest_of_step(src, STEPS + mine, p)
                    if t > 1:
                        mid = [mixed[p, mine, :, tile_at(s)] for s in range(groups)]
                    ahead = shifted(mid)
                    behind = [pltpu.roll(v, 1, 1) for v in mid]
                    for s in range(groups):
                        right = jnp.where(at_last, ahead[(s + 1) % groups], ahead[s])
                        left = jnp.where(at_first, behind[(s - 1) % groups], behind[s])
                        value = out[s] + (ratio * right_part * right + ratio * left_part * left)
                        if t < STEPS:
                            dst[p, STEPS + mine, :, tile_at(s)] = out[s]
                            mixed[p, mine, :, tile_at(s)] = value
                            continue
                        value = value * scale
                        mixed[p, mine, :, tile_at(s)] = value
                        for g, (start, count) in enumerate(splits):
                            if start <= p < start + count:
                                at = pl.ds(pl.multiple_of(mine * TILE, TILE), TILE)
                                out_refs[g][p - start, s, at, :] = value.astype(jnp.bfloat16)
            return 0

        if reach:
            lax.fori_loop(0, reach, edge_rows, 0)
        lax.fori_loop(0, rows // pace, own_rows, 0)

    column = lax.broadcasted_iota(jnp.int32, (block_cols, LANES), 0)

    def observe(i, _):
        for k in range(pace):
            y = pace * i + k
            for b in range(blocks):
                cell = small_refs[b][pl.ds(y, 1), :].astype(jnp.int32)
                plane = cell // block_cols
                pick = jnp.where(column == cell - plane * block_cols, 1.0, 0.0).astype(jnp.bfloat16)
                start = (lax.axis_index("member") + b) % blocks * block_cols
                part = mixed[:, y, :, pl.ds(pl.multiple_of(start, LANES), block_cols)]
                part = part.reshape(planes * TILE, block_cols).astype(jnp.bfloat16)
                found = jnp.dot(part, pick, preferred_element_type=jnp.float32).reshape(planes, TILE, LANES)
                total = jnp.zeros((TILE, LANES), jnp.float32)
                for p in range(planes):
                    total = jnp.where(plane == p, found[p], total)
                obs_ref[0, y, b] = total.astype(jnp.bfloat16)
        return 0

    lax.fori_loop(0, rows // pace, observe, 0)


def stencil(turned, first, second, coef, smalls, held, tile, local, splits, fields, rows, levels, cols):
    planes = fields * levels
    blocks = len(smalls)
    tiles = coef.shape[0] // TILE
    outs = [jax.ShapeDtypeStruct((count, cols // LANES, rows * TILE, LANES), jnp.bfloat16) for _, count in splits]
    observed = jax.ShapeDtypeStruct((tiles, rows, blocks, TILE, LANES), jnp.bfloat16)
    room = pltpu.VMEM((planes, rows + 2 * STEPS, TILE, cols), jnp.float32)
    far = pl.BlockSpec(memory_space=pltpu.HBM)

    near = pl.BlockSpec(memory_space=pltpu.VMEM)
    in_specs = [near if tile < HEAD else far, near, near, pl.BlockSpec((TILE, fields), lambda i: (tile, 0))]
    in_specs += [near] * len(smalls)
    args = [turned, first, second, coef, *(near_core(small) for small in smalls)]
    aliases = {}
    if held is not None:
        aliases = {len(args): len(splits)}
        in_specs.append(far)
        args.append(held)
    return pl.pallas_call(
        lambda *refs: stencil_kernel(fields, rows, levels, cols, blocks, splits, local, len(aliases), *refs),
        grid=(1,),
        in_specs=in_specs,
        out_specs=[pl.BlockSpec(out.shape, lambda i: (0, 0, 0, 0)) for out in outs]
        + [pl.BlockSpec((1, *observed.shape[1:]), lambda i: (tile, 0, 0, 0, 0))],
        out_shape=[*outs, observed],
        scratch_shapes=[
            room,
            room,
            pltpu.VMEM((planes, rows, TILE, cols), jnp.float32),
            pltpu.SemaphoreType.DMA,
        ],
        input_output_aliases=aliases,
        compiler_params=pltpu.CompilerParams(vmem_limit_bytes=KERNEL_VMEM),
        name="stencil",
    )(*args)


def product(a, b):
    a_high = a.astype(jnp.bfloat16)
    a_low = (a - a_high.astype(jnp.float32)).astype(jnp.bfloat16)
    b_high = b.astype(jnp.bfloat16)
    b_low = (b - b_high.astype(jnp.float32)).astype(jnp.bfloat16)
    left = jnp.concatenate([a_high, a_low], axis=1)
    right = jnp.concatenate(
        [jnp.concatenate([b_high, b_low], axis=1), jnp.concatenate([b_high, jnp.zeros_like(b_low)], axis=1)], axis=0
    )
    both = jnp.dot(left, right, preferred_element_type=jnp.float32)
    return both[:, :b.shape[1]] + both[:, b.shape[1]:]


def solve_kernel(rows, members, ensemble, pairs, table_ref, own_ref, near_ref, far_ref, upper_ref, lower_ref, sum_ref, wide, ys, zs, ms, gs, scales, direct):
    width = 2 * ensemble
    count = rows * pairs
    odd = place_in_pair() == 1

    def fill(r, _):
        for q in range(pairs):
            near = near_ref[r, q].astype(jnp.float32)
            far = far_ref[r, q].astype(jnp.float32)
            wide[r, q] = jnp.where(odd, near, far)
            wide[rows + r, q] = own_ref[r, q]
            wide[2 * rows + r, q] = jnp.where(odd, far, near)
        return 0

    lax.fori_loop(0, rows, fill, 0)

    lane = lax.broadcasted_iota(jnp.int32, (ensemble, width), 1)
    first = lane < ensemble
    eye = jnp.where(
        lax.broadcasted_iota(jnp.int32, (width, width), 0) == lax.broadcasted_iota(jnp.int32, (width, width), 1), 1.0, 0.0
    )
    first_row = lax.broadcasted_iota(jnp.int32, (TILE, width), 1) < ensemble

    def localize(i, _):
        for y, q in ((2 * i + k, q) for k in range(2) for q in range(pairs)):
            local = jnp.zeros(wide.shape[2:], jnp.float32)
            for d in range(-HALO, HALO + 1):
                local = local + table_ref[d + HALO, y] * wide[rows + y + d, q]
            gram = local[:ensemble]
            amat = jnp.concatenate([jnp.where(first, gram, 0.0), jnp.where(first, 0.0, gram)], axis=0) + (ensemble - 1.0) * eye
            square = amat * amat
            tops = jnp.sqrt(jnp.sum(square[:ensemble], axis=(0, 1), keepdims=True))
            ends = jnp.sqrt(jnp.sum(square[ensemble:], axis=(0, 1), keepdims=True))
            part = jnp.concatenate(
                [jnp.broadcast_to(1.0 / tops, (ensemble, width)), jnp.broadcast_to(1.0 / ends, (ensemble, width))], axis=0
            )
            at = y * pairs + q
            ys[at] = amat * part
            gs[at] = local[ensemble:ensemble + TILE]
            scales[at] = jnp.where(first_row, tops, ends)
        return 0

    lax.fori_loop(0, rows // 2, localize, 0)

    pace = 8 if count % 8 == 0 else 1

    def each(work):
        def some(i, _):
            for k in range(pace):
                work(pace * i + k)
            return 0

        lax.fori_loop(0, count // pace, some, 0)

    for step_idx in range(NS_STEPS):
        def middle(i):
            ms[i] = 1.5 * eye - 0.5 * (product(zs[i], ys[i]) if step_idx else ys[i])

        def apply(i):
            if step_idx < NS_STEPS - 1:
                ys[i] = product(ys[i], ms[i])
            zs[i] = product(ms[i], zs[i]) if step_idx else ms[i]

        each(middle)
        each(apply)

    def weigh(i, total):
        for y, q in ((2 * i + k, q) for k in range(2) for q in range(pairs)):
            at = y * pairs + q
            z, scale = zs[at], scales[at]
            mean = (product(product(gs[at], z), z) / scale)[:1]
            wpert = z[:members] + z[ensemble:ensemble + members]
            weights = wpert * (math.sqrt(ensemble - 1.0) / jnp.sqrt(scale))[:1] + mean
            total = total + weights
            here = first[:members]
            low = jnp.sum(jnp.where(here, weights, 0.0), axis=1, keepdims=True)
            high = jnp.sum(jnp.where(here, 0.0, weights), axis=1, keepdims=True)
            direct[q, pl.ds(y, members, stride=rows), :] = weights + (1.0 - jnp.where(here, low, high)) / ensemble
        return total

    sum_ref[...] = lax.fori_loop(0, rows // 2, weigh, jnp.zeros((members, width), jnp.float32))

    depth = ensemble * rows
    column = lax.broadcasted_iota(jnp.int32, (width, depth), 1)
    member = column // (rows * TILE) * TILE + column % TILE
    entry = lax.broadcasted_iota(jnp.int32, (width, depth), 0)
    mine = lax.broadcasted_iota(jnp.int32, (members * rows, depth), 0) % rows
    theirs = lax.broadcasted_iota(jnp.int32, (members * rows, depth), 1) // TILE % rows
    keep = mine == theirs
    for half in range(2):
        place = jnp.where(entry == member + half * ensemble, 1.0, 0.0).astype(jnp.bfloat16)
        for q in range(pairs):
            w = direct[q]
            high = w.astype(jnp.bfloat16)
            low = (w - high.astype(jnp.float32)).astype(jnp.bfloat16)
            for part, ref in ((high, upper_ref), (low, lower_ref)):
                spread = jnp.dot(part, place, preferred_element_type=jnp.float32)
                ref[2 * q + half] = jnp.where(keep, spread, 0.0).astype(jnp.bfloat16)


def solve(table, own, near, far, members, ensemble):
    rows, pairs, tall, width = own.shape
    count = rows * pairs
    out = pltpu.VMEM((2 * pairs, members * rows, ensemble * rows), jnp.bfloat16)
    square = pltpu.VMEM((count, width, width), jnp.float32)
    line = pltpu.VMEM((count, TILE, width), jnp.float32)
    smem = pl.BlockSpec(memory_space=pltpu.SMEM)
    vmem = pl.BlockSpec(memory_space=pltpu.VMEM)
    return pl.pallas_call(
        lambda *refs: solve_kernel(rows, members, ensemble, pairs, *refs),
        in_specs=[smem, vmem, vmem, vmem],
        out_specs=[vmem] * 3,
        out_shape=[out, out, jax.ShapeDtypeStruct((members, width), jnp.float32)],
        scratch_shapes=[
            pltpu.VMEM((3 * rows, pairs, tall, width), jnp.float32),
            square, square, square, line, line,
            pltpu.VMEM((pairs, members * rows, width), jnp.float32),
        ],
        compiler_params=pltpu.CompilerParams(vmem_limit_bytes=KERNEL_VMEM),
        name="solve",
    )(table, own, near, far)


def update_kernel(members, rows, cols, blocks, offsets, upper, lower, *rest):
    pieces, out_ref = rest[:len(offsets)], rest[-1]
    plane, b = pl.program_id(0), pl.program_id(1)
    groups = cols // blocks // LANES
    columns = []
    for s in range(groups):
        columns.append(jnp.concatenate([piece[at + plane, b * groups + s] for piece, at in zip(pieces, offsets)], axis=0))
    x = jnp.concatenate(columns, axis=1) if groups > 1 else columns[0]
    mine = (b + blocks - lax.axis_index("member")) % blocks
    total = jnp.dot(upper[mine], x, preferred_element_type=jnp.float32)
    total = total + jnp.dot(lower[mine], x, preferred_element_type=jnp.float32)
    out_ref[:, 0] = total.reshape(members, rows, groups * LANES).astype(jnp.bfloat16)


def update(upper, lower, pieces, offsets, start, count, held, members, planes, rows, cols):
    blocks = upper.shape[0]
    in_specs = [pl.BlockSpec(memory_space=pltpu.VMEM)] * (2 + len(pieces))
    args = [upper, lower, *(near_core(piece) for piece in pieces)]
    aliases = {}
    if held is not None:
        aliases = {len(args): 0}
        in_specs.append(pl.BlockSpec(memory_space=pl.ANY))
        args.append(held)
    return pl.pallas_call(
        lambda *refs: update_kernel(members, rows, cols, blocks, offsets, *refs),
        grid=(count, blocks),
        in_specs=in_specs,
        out_specs=pl.BlockSpec((members, 1, rows, cols // blocks), lambda i, b: (0, start + i, 0, b)),
        out_shape=jax.ShapeDtypeStruct((members, planes, rows, cols), jnp.bfloat16),
        input_output_aliases=aliases,
        compiler_params=pltpu.CompilerParams(vmem_limit_bytes=KERNEL_VMEM),
        name="update",
    )(*args)


def near_core(array):
    return pltpu.with_memory_space_constraint(array, pltpu.VMEM)


def from_member(array, shift):
    count = lax.axis_size("member")
    return lax.ppermute(array, "member", [((i + shift) % count, i) for i in range(count)])


def all_members(array):
    return [array] + [from_member(array, shift) for shift in range(1, lax.axis_size("member"))]


def swap_one(array):
    return lax.ppermute(array, "slab", [(i, i ^ 1) for i in range(lax.axis_size("slab"))])


def swap_two(array):
    pairs = [(i, i + 1) for i in range(1, lax.axis_size("slab") - 1, 2)]
    return lax.ppermute(array, "slab", pairs + [(j, i) for i, j in pairs])


def groups_of(planes):
    sizes = [2] * (planes // 2 - 1) + [1, 1] if planes % 2 == 0 else [1] * planes
    return [(sum(sizes[:i]), size) for i, size in enumerate(sizes)]


def cycle(prior_ensemble_fields, params, influence, obs_cell, obs_value, obs_prec, cutoff):
    highest = lax.Precision.HIGHEST
    fine_grain = lax.Precision.HIGH
    members, fields, rows, levels, cols = prior_ensemble_fields.shape
    planes = fields * levels
    tiles = members // TILE
    devices = lax.axis_size("member")
    slabs = lax.axis_size("slab")
    ensemble = members * devices
    dims = (fields, rows, levels, cols)
    x2 = prior_ensemble_fields.reshape(members * fields * rows * levels * (cols // LANES), LANES)

    head = min(HEAD, tiles)
    *packed, turned = pack(x2, 0, head, True, *dims)
    turned = [(turned, i) for i in range(head)]
    if tiles > head:
        *more, others = pack(x2, head, tiles - head, False, *dims)
        packed += more
        others = pltpu.with_memory_space_constraint(others, pltpu.HBM)
        turned += [(others, i) for i in range(tiles - head)]
    edges = []
    for i in range(tiles):
        edges.append((near_core(swap_one(packed[2 * i])), near_core(swap_two(packed[2 * i + 1]))))

    columns = obs_cell.shape[2]
    npar = params.shape[1]
    own_small = jnp.concatenate(
        [obs_cell[:, 0].astype(jnp.float32), obs_value[:, 0], obs_prec[:, 0]]
        + [jnp.pad(params.T, ((0, -npar % TILE), (0, columns - members)))]
    )
    smalls = all_members(own_small)
    every_param = jnp.concatenate([small[3 * rows:3 * rows + npar, :members].T for small in smalls])
    values = jnp.stack([small[rows:2 * rows] for small in smalls], axis=1)
    precs = jnp.stack([small[2 * rows:3 * rows] for small in smalls], axis=1)

    coef = jnp.dot(params, influence.astype(jnp.float32), precision=highest)

    fine = groups_of(planes)
    forecasts, own_obs = [], None
    for i in range(tiles):
        splits = [(0, planes)]
        if i == tiles - 1:
            splits = fine
        elif i == 1:
            splits = [(0, fine[-2][0]), (fine[-2][0], planes - fine[-2][0])]
        fields_here, local = turned[i]
        *outs, own_obs = stencil(fields_here, *edges[i], coef, smalls, own_obs, i, local, splits, *dims)
        forecasts.append((splits, outs))
    ens_obs = jnp.stack([jnp.roll(array, shift, axis=2) for shift, array in enumerate(all_members(own_obs))])
    sent = []
    for splits, outs in forecasts:
        arrays = []
        for out in outs:
            arrays.append(all_members(out))
        sent.append((splits, arrays))

    ens_obs = ens_obs.transpose(2, 3, 0, 1, 4, 5).reshape(rows, devices, ensemble, LANES).astype(jnp.float32)
    ybar = jnp.mean(ens_obs, axis=2, keepdims=True)
    ypert = ens_obs - ybar
    weighted = precs * (values - ybar[:, :, 0])
    gram = jnp.einsum("rbeo,rbfo->rbef", ypert * precs[:, :, None], ypert, precision=fine_grain)
    gvec = jnp.einsum("rbeo,rbo->rbe", ypert, weighted, precision=highest)
    empty = jnp.zeros((rows, devices, TILE - 1, ensemble), jnp.float32)
    stacked = jnp.concatenate([gram, gvec[:, :, None, :], empty], axis=2)
    stacked = jnp.concatenate([stacked[:, 0::2], stacked[:, 1::2]], axis=3)
    rounded = stacked.astype(jnp.bfloat16)
    near, far = near_core(swap_one(rounded)), near_core(swap_two(rounded))
    radius = cutoff.astype(jnp.float32)
    distance = jnp.abs(jnp.arange(-HALO, HALO + 1, dtype=jnp.float32))[:, None]
    table = jnp.maximum(0.0, 1.0 - distance / (radius + 1.0))
    upper, lower, weight_rows = solve(table, near_core(stacked), near, far, members, ensemble)

    analysis = None
    for start, count in fine:
        pieces, offsets = [], []
        for r in range(devices):
            for splits, arrays in sent:
                part = max(k for k, (at, _) in enumerate(splits) if at <= start)
                pieces.append(arrays[part][r])
                offsets.append(start - splits[part][0])
        analysis = update(upper, lower, pieces, offsets, start, count, analysis, members, planes, rows, cols)
    analysis = analysis.reshape(members, fields, levels, rows, cols).transpose(0, 1, 3, 2, 4)

    pbar = jnp.mean(every_param, axis=0)
    ppert = every_param - pbar
    weight_rows = weight_rows[:, :ensemble] + weight_rows[:, ensemble:]
    part = jnp.einsum("jk,ej->ke", ppert, weight_rows, precision=highest)
    step = 1
    while step < slabs:
        ways = min(4, slabs // step)
        part = sum(
            (lax.ppermute(part, "slab", [(i, i ^ (k * step)) for i in range(slabs)]) for k in range(1, ways)), part
        )
        step *= ways
    total = part / (rows * slabs * devices)
    param_analysis = pbar + total.T
    return (analysis, param_analysis)


def solution(mesh):
    in_specs = (
        P("member", None, "slab", None, None),
        P("member", None),
        P(),
        P("slab", "member", None),
        P("slab", "member", None),
        P("slab", "member", None),
        P("slab"),
    )
    out_specs = (P("member", None, "slab", None, None), P("member", None))
    return jax.shard_map(cycle, mesh=mesh, in_specs=in_specs, out_specs=out_specs, check_vma=False)
```
